256 devices in a mesh: slab: 8 (over y, core), trace: 32 (over x, z).
Axes of the slice: x: 4, y: 4, z: 8, core: 2. Of those that a mesh axis runs over, the one named last changes fastest.
Arguments:
- near_tiles: float32 [8, 2, 2, 768, 24576], P('slab', None, None, None, 'trace'), may hold values from -0.078125 to 0.078125
- near_side: int32 [8, 32], P('slab', 'trace'), may hold values from -1 to 1, as said below
- skeleton: int32 [8, 32, 64], P('slab', 'trace'), may hold values from 0 to 767, as said below
- far_coupling: float32 [8, 2, 2048, 2048], P('slab', None, 'trace'), may hold values from -0.0625 to 0.0625
- far_basis: float32 [8, 2, 64, 24576], P('slab', None, None, 'trace'), may hold values from -0.5 to 0.5
- sources: float32 [8, 2, 1, 16, 24576], P('slab', None, None, None, 'trace'), may hold values from -200 to 200
Outputs:
- traces: float32 [8, 2, 1, 16, 24576], P('slab', None, None, None, 'trace')
The draws below stay inside these ranges and needn't reach their ends.
Inputs may be any that keep to these rules, and one draw needn't show every extreme that they name: `near_side`: each entry is -1 or 1, so that the second near tile lies in a block next to the row's own block; it is 1 for the first block and -1 for the last. `skeleton`: the 64 positions of one block are distinct.
All inputs are finite; a program needn't handle non-finite values.
Results may differ from the reference program's by a relative error of at most 0.0001.
Values sent between devices are 32-bit elements; how exact they have to be, the bound alone decides.
A program may use at most 128 MiB of HBM per device.

```python
import math
import jax
import jax.numpy as jnp
from jax import lax

TILE = 768
RANK = 64
NEAR = 2
MB = 1
B = 16
BLOCKS = 32
N = 24576
N_SLAB = 8


def draw_near_side(key, part):
    coin = jax.random.randint(key, (N_SLAB, BLOCKS), 0, 2).astype(jnp.int32)
    offsets = 2 * coin - 1
    column = jnp.arange(BLOCKS, dtype=jnp.int32)[None, :]
    offsets = jnp.where(column == 0, 1, offsets)
    offsets = jnp.where(column == BLOCKS - 1, -1, offsets)
    return offsets.astype(jnp.int32)


def draw_skeleton(key, part):
    scores = jax.random.randint(key, (N_SLAB, BLOCKS, TILE), 0, 1 << 20).astype(jnp.int32) * TILE + jnp.arange(TILE, dtype=jnp.int32)
    order = jnp.argsort(scores, axis=-1)
    return order[..., :RANK].astype(jnp.int32)


def draw_sources(key, part):
    key_col, key_row, key_base = jax.random.split(key, 3)
    position = jnp.arange(N, dtype=jnp.float32) / N
    rough = jnp.exp(jax.random.uniform(key_col, (N_SLAB, 1, 1, 1, N), jnp.float32, 0.0, math.log(3.3)))
    col_scale = jnp.power(3.0, position) * rough
    row_scale = jnp.exp(jax.random.uniform(key_row, (N_SLAB, 1, MB, B, 1), jnp.float32, 0.0, math.log(5.0)))
    shape_all = (N_SLAB, 2, MB, B, N)
    base = jnp.clip(jax.random.normal(key_base, shape_all, jnp.float32), -4.0, 4.0)
    return (base * col_scale * row_scale).astype(jnp.float32)


def levels(key, dims, cuts, least, high):
    gain = 1.0
    for dim, parts in cuts:
        heights = jax.random.uniform(jax.random.fold_in(jax.random.fold_in(key, 6), dim), (parts,), jnp.float32, least / len(cuts), high / len(cuts))
        gain = gain * jnp.repeat(jnp.exp(heights), dims[dim] // parts).reshape((-1,) + (1,) * (len(dims) - 1 - dim))
    return gain


def centred(stream_key, dims, deviation, limit, cuts=(), kind=jnp.bfloat16):
    loudness = levels(stream_key, dims, cuts, -0.22, 0.18) if cuts else 1.0
    drawn = jax.random.normal(stream_key, dims, jnp.float32) * deviation * loudness
    return jnp.minimum(jnp.maximum(drawn, -limit), limit).astype(kind)


def setup_inputs(seed: int = 0) -> dict:
    streams_of = jax.random.split(jax.random.key(seed), 7)
    near_tiles = centred(streams_of[0], (N_SLAB, NEAR, 2, TILE, N), (4 * NEAR * TILE) ** -0.5, 0.078125, ((0, 8), (4, 32)), jnp.float32)
    near_side = draw_near_side(jax.random.fold_in(streams_of[6], 71), 0)
    skeleton = draw_skeleton(jax.random.fold_in(streams_of[6], 71), 0)
    far_coupling = centred(streams_of[3], (N_SLAB, 2, BLOCKS * RANK, BLOCKS * RANK), (4 * BLOCKS * RANK) ** -0.5, 0.0625, ((0, 8), (2, 32)), jnp.float32)
    far_basis = centred(streams_of[4], (N_SLAB, 2, RANK, N), (2 * RANK) ** -0.5, 0.5, ((0, 8), (3, 32)), jnp.float32)
    sources = draw_sources(jax.random.fold_in(streams_of[6], 71), 0)
    return {"near_tiles": near_tiles, "near_side": near_side, "skeleton": skeleton, "far_coupling": far_coupling, "far_basis": far_basis, "sources": sources}


exact_mode = lax.Precision.HIGHEST
small_eps = 1e-06

def block_product(form, left_re, left_im, right_re, right_im):
    real_part = jnp.einsum(form, left_re, right_re, precision=exact_mode) - jnp.einsum(form, left_im, right_im, precision=exact_mode)
    imag_part = jnp.einsum(form, left_re, right_im, precision=exact_mode) + jnp.einsum(form, left_im, right_re, precision=exact_mode)
    return (real_part, imag_part)

def reference(near_tiles, near_side, skeleton, far_coupling, far_basis, sources):
    row_count = MB * B
    block_ids = jnp.arange(BLOCKS, dtype=jnp.int32)
    owner_ids = jnp.arange(BLOCKS * RANK, dtype=jnp.int32) // RANK
    trace_in = jnp.zeros((2, row_count, BLOCKS, TILE), jnp.float32)
    results = []
    for slab_idx in range(N_SLAB):
        tile_set = near_tiles[slab_idx].reshape(NEAR, 2, TILE, BLOCKS, TILE)
        offsets = near_side[slab_idx].astype(jnp.int32)
        beside_in = jnp.take(trace_in, block_ids + offsets, axis=2)
        own_re, own_im = block_product('abi,ibo->abo', trace_in[0], trace_in[1], tile_set[0, 0], tile_set[0, 1])
        next_re, next_im = block_product('abi,ibo->abo', beside_in[0], beside_in[1], tile_set[1, 0], tile_set[1, 1])
        picked = jnp.take_along_axis(trace_in, skeleton[slab_idx][None, None], axis=3).reshape(2, row_count, BLOCKS * RANK)
        keep_mask = ((owner_ids[None, :] != block_ids[:, None]) & (owner_ids[None, :] != (block_ids + offsets)[:, None])).astype(jnp.float32)
        masked = picked[:, :, None, :] * keep_mask[None, None]
        coupling = far_coupling[slab_idx].reshape(2, BLOCKS, RANK, BLOCKS * RANK)
        coef_re, coef_im = block_product('abj,bkj->abk', masked[0], masked[1], coupling[0], coupling[1])
        basis = far_basis[slab_idx].reshape(2, RANK, BLOCKS, TILE)
        far_re, far_im = block_product('abk,kbo->abo', coef_re, coef_im, basis[0], basis[1])
        source = sources[slab_idx].reshape(2, row_count, BLOCKS, TILE)
        updated = jnp.stack([own_re + next_re + far_re, own_im + next_im + far_im]) + source
        trace_in = updated
        energy = lax.optimization_barrier(jnp.sum(updated * updated, axis=(0, 2, 3))) / (2 * BLOCKS * TILE)
        normed = updated / jnp.sqrt(energy + small_eps)[None, :, None, None]
        results.append(normed.reshape(2, MB, B, BLOCKS * TILE))
    return jnp.stack(results)
```

```python
import functools

import jax
import jax.numpy as jnp
from jax import lax
from jax.experimental import pallas as pl
from jax.experimental.pallas import tpu as pltpu
from jax.sharding import PartitionSpec as P

MESH = pl.DeviceIdType.MESH
F32 = jnp.float32
BF16 = jnp.bfloat16
small_eps = 1e-06


def halves(x):
    hi = x.astype(BF16)
    lo = (x - hi.astype(F32)).astype(BF16)
    return hi, lo


def thirds(x):
    hi = x.astype(BF16)
    rest = x - hi.astype(F32)
    mid = rest.astype(BF16)
    lo = (rest - mid.astype(F32)).astype(BF16)
    return hi, mid, lo


def mm(a, b):
    return jnp.dot(a, b, preferred_element_type=F32)


def outward(k, n):
    return (n // 2 + ((k + 1) // 2) * (1 - 2 * (k % 2))) % n


def kernel(
    sizes,
    near_hbm,
    side_ref,
    skel_ref,
    coup_hbm,
    basis_hbm,
    src_hbm,
    out_ref,
    near_f,
    near_hi,
    near_lo,
    coup_f,
    basis_f,
    basis_w,
    src_v,
    skel_out,
    skel_next,
    pick_w,
    wp,
    wc,
    u_in,
    u_out,
    p_in,
    p_out,
    e_in,
    e_out,
    w_sem,
    skel_sem,
    u_send,
    u_recv,
    p_send,
    p_recv,
    e_send,
    e_recv,
):
    ns, nt, nx, nz = sizes
    tile = src_v.shape[2]
    rows = src_v.shape[1]
    rank = skel_ref.shape[1]
    slab = lax.axis_index("slab")
    me = lax.axis_index("trace")
    my_x, my_z = me // nz, me % nz
    has_next = slab < ns - 1
    has_prev = slab > 0
    lane = lax.broadcasted_iota(jnp.int32, (rank, 2 * rank), 1)
    first = lane < rank

    loads = [
        pltpu.make_async_copy(src_hbm, src_v, w_sem.at[0]),
        pltpu.make_async_copy(basis_hbm, basis_f, w_sem.at[1]),
        pltpu.make_async_copy(coup_hbm, coup_f, w_sem.at[2]),
    ]
    for slot in range(2):
        for part in range(2):
            loads.append(
                pltpu.make_async_copy(
                    near_hbm.at[slot, part], near_f.at[slot, part], w_sem.at[3 + 2 * slot + part]
                )
            )
    for load in loads:
        load.start()

    barrier = pltpu.get_barrier_semaphore()

    def greet(s, t):
        pl.semaphore_signal(barrier, inc=1, device_id=(s, t), device_id_type=MESH)

    @pl.when(has_next)
    def _():
        greet(slab + 1, me)

    @pl.when(has_prev)
    def _():
        @pl.loop(0, nt)
        def _(k):
            greet(slab - 1, (me + nt // 2 + k) % nt)

    @pl.loop(1, nt)
    def _(k):
        greet(slab, (me + k) % nt)

    twin = jnp.concatenate([skel_ref[...], skel_ref[...]], axis=1)
    skel_out[...] = jnp.broadcast_to(twin, skel_out.shape)

    pl.semaphore_wait(
        barrier, nt - 1 + nt * has_next.astype(jnp.int32) + has_prev.astype(jnp.int32)
    )

    skel_copy = pltpu.make_async_remote_copy(
        src_ref=skel_out,
        dst_ref=skel_next,
        send_sem=skel_sem.at[0],
        recv_sem=skel_sem.at[1],
        device_id=(slab - 1, me),
        device_id_type=MESH,
    )

    @pl.when(has_prev)
    def _():
        skel_copy.start()

    def send_u():
        for i, shift in enumerate((0, 1, nt - 1)):
            pltpu.make_async_remote_copy(
                src_ref=u_out,
                dst_ref=u_in.at[i],
                send_sem=u_send.at[i],
                recv_sem=u_recv.at[i],
                device_id=(slab + 1, (me + shift) % nt),
                device_id_type=MESH,
            ).start()

    def send_p():
        @pl.loop(0, nt)
        def _(k):
            dz, dx = outward(k // nx, nz), outward(k % nx, nx)
            to = ((my_x + dx) % nx) * nz + (my_z + dz) % nz
            pltpu.make_async_remote_copy(
                src_ref=p_out,
                dst_ref=p_in.at[dz, my_x],
                send_sem=p_send,
                recv_sem=p_recv.at[dz],
                device_id=(slab + 1, to),
                device_id_type=MESH,
            ).start()

    def pick(x):
        parts = mm(jnp.concatenate(thirds(x), axis=0), pick_w[...])
        n = 2 * rows
        got = parts[:n] + parts[n : 2 * n] + parts[2 * n :]
        return jnp.where(first[:rows], got[:rows], got[rows:])

    @pl.when(has_next)
    def _():
        skel_copy.wait_recv()
        place = lax.broadcasted_iota(jnp.int32, (tile, 2 * rank), 0)
        pick_w[...] = (place == skel_next[:1, :]).astype(BF16)

    @pl.when(jnp.logical_not(has_next))
    def _():
        pick_w[...] = jnp.zeros_like(pick_w)

    loads[0].wait()

    @pl.when(slab == 0)
    def _():
        u_out[...] = src_v[...]
        p_out[...] = pick(src_v[...].reshape(2 * rows, tile))
        send_p()
        send_u()
        u_in[...] = jnp.zeros_like(u_in)
        p_in[...] = jnp.zeros_like(p_in)

    side = side_ref[...]

    loads[1].wait()
    b_re, b_im = basis_f[0], basis_f[1]
    top = jnp.concatenate([b_re, -b_im], axis=0)
    bottom = jnp.concatenate([b_im, b_re], axis=0)
    for i, m in enumerate((top, bottom)):
        hi, lo = halves(m)
        basis_w[: 2 * rank, i * tile : (i + 1) * tile] = hi
        basis_w[2 * rank :, i * tile : (i + 1) * tile] = lo
    picked = mm(jnp.concatenate(thirds(jnp.concatenate([b_re, b_im], axis=0)), axis=0), pick_w[...])
    n = 2 * rank
    picked = picked[:n] + picked[n : 2 * n] + picked[2 * n :]
    s_re, s_im = picked[:rank], picked[rank:]
    s_mat = jnp.concatenate([jnp.where(first, s_re, s_im), jnp.where(first, -s_im, s_re)], axis=0)
    s_hi, s_lo = halves(s_mat)
    s_w = jnp.concatenate([s_hi, s_lo], axis=1)
    loads[2].wait()

    @pl.loop(0, nt // 2)
    def _(t):
        at = pl.ds(pl.multiple_of(t * 2 * rank, 2 * rank), 2 * rank)
        re, im = coup_f[0, :, at], coup_f[1, :, at]
        re_r, im_r = pltpu.roll(re, rank, 1), pltpu.roll(im, rank, 1)
        for odd in range(2):
            c = 2 * t + odd
            if odd == 0:
                a = jnp.concatenate([jnp.where(first, re, -im_r), jnp.where(first, im, re_r)], axis=0)
            else:
                a = jnp.concatenate([jnp.where(first, re_r, -im), jnp.where(first, im_r, re)], axis=0)
            keep = jnp.logical_and(side + me != c, me != c).astype(F32)
            a = (a * keep).T
            hi, lo = halves(a)
            prod = mm(jnp.concatenate([hi, lo], axis=0), s_w)
            w = prod[:n, :n] + prod[n:, :n] + prod[:n, n:]
            w_hi, w_lo = halves(w)
            cx, cz = c // nz, c % nz
            out_at = pl.ds(pl.multiple_of(cx * n, n), n)
            wp[cz, out_at, :n] = w_hi
            wp[cz, out_at, n:] = w_lo
            wc[cz, out_at, :n] = hi
            wc[cz, out_at, n:] = lo

    for slot in range(2):
        for part in range(2):
            loads[3 + 2 * slot + part].wait()

            @pl.loop(0, tile // 32)
            def _(i):
                at = pl.ds(pl.multiple_of(i * 32, 32), 32)
                hi, lo = halves(near_f[slot, part, at, :])
                near_hi[slot, part, at, :] = hi
                near_lo[slot, part, at, :] = lo

    @pl.when(has_prev)
    def _():
        for i in range(3):
            pltpu.make_async_copy(u_in.at[i], u_in.at[i], u_recv.at[i]).wait()

    own = u_in[0].reshape(2 * rows, tile)
    beside = jnp.where(
        jnp.broadcast_to(side, (2 * rows, tile)) > 0,
        u_in[2].reshape(2 * rows, tile),
        u_in[1].reshape(2 * rows, tile),
    )
    sums = []
    lhs = [halves(own), halves(beside)]
    for part in range(2):
        total = None
        for slot in range(2):
            hi, lo = lhs[slot]
            both = mm(jnp.concatenate([hi, lo], axis=0), near_hi[slot, part])
            term = both[: 2 * rows] + both[2 * rows :] + mm(hi, near_lo[slot, part])
            total = term if total is None else total + term
        sums.append(total)
    n_re = sums[0][:rows] - sums[1][rows:] + src_v[0]
    n_im = sums[1][:rows] + sums[0][rows:] + src_v[1]
    u_new = jnp.concatenate([n_re, n_im], axis=0)
    ahead = pick(u_new)

    acc_p = jnp.zeros((2 * rows, 2 * n), F32)
    acc_c = jnp.zeros((2 * rows, 2 * n), F32)
    order = [int(outward(k, nz)) for k in range(nz)][::-1]
    for i, dz in enumerate(order):

        @pl.when(has_prev)
        def _():
            pltpu.make_async_copy(p_in.at[dz], p_in.at[dz], p_recv.at[dz]).wait()

        got = jnp.concatenate([p_in[dz, x] for x in range(nx)], axis=1)
        got = jnp.concatenate(halves(got), axis=0)
        cz = (my_z - dz + nz) % nz
        acc_p += mm(got, wp[cz])
        if i == nz - 1:
            fold = acc_p[:rows] + acc_p[rows:]
            p_new = ahead + fold[:, :n] + fold[:, n:]

            @pl.when(jnp.logical_and(has_prev, has_next))
            def _():
                p_out[...] = p_new
                send_p()

        acc_c += mm(got, wc[cz])
    fold = acc_c[:rows] + acc_c[rows:]
    coef = fold[:, :n] + fold[:, n:]
    c_hi, c_lo = halves(coef)
    lhs_c = jnp.concatenate(
        [jnp.concatenate([c_hi, c_hi], axis=1), jnp.concatenate([c_lo, c_lo], axis=1)], axis=0
    )
    far = mm(lhs_c, basis_w[...])
    far = far[:rows] + far[rows:]
    u_re = n_re + far[:, :tile]
    u_im = n_im + far[:, tile:]

    @pl.when(has_prev)
    def _():
        u_out[0] = u_re
        u_out[1] = u_im

    @pl.when(jnp.logical_and(has_prev, has_next))
    def _():
        send_u()

    part_sum = jnp.sum(u_re * u_re + u_im * u_im, axis=1, keepdims=True)
    diag = (
        lax.broadcasted_iota(jnp.int32, (rows, 128), 0)
        == lax.broadcasted_iota(jnp.int32, (rows, 128), 1)
    ).astype(F32)
    e_out[...] = jnp.sum(part_sum * diag, axis=0, keepdims=True)

    @pl.loop(1, nt)
    def _(k):
        rel = outward(k - 1, nt - 1) + 1
        pltpu.make_async_remote_copy(
            src_ref=e_out,
            dst_ref=e_in.at[rel - 1],
            send_sem=e_send,
            recv_sem=e_recv,
            device_id=(slab, (me + rel) % nt),
            device_id_type=MESH,
        ).start()

    pltpu.make_async_copy(e_in, e_in, e_recv).wait()
    total = e_out[...] + jnp.sum(e_in[...], axis=0)
    energy = jnp.sum(total * diag, axis=1, keepdims=True) / (2 * tile * nt)
    scale = 1.0 / jnp.sqrt(energy + small_eps)
    out_ref[0] = u_re * scale
    out_ref[1] = u_im * scale

    pltpu.make_async_copy(e_in, e_in, e_send).wait()

    @pl.when(has_next)
    def _():
        for i in range(3):
            pltpu.make_async_copy(u_out, u_out, u_send.at[i]).wait()
        pltpu.make_async_copy(p_in, p_in, p_send).wait()

    @pl.when(has_prev)
    def _():
        skel_copy.wait_send()


def solution(mesh):
    ns, nt = mesh.shape["slab"], mesh.shape["trace"]
    nz = 8 if nt % 8 == 0 else nt // 2
    nx = nt // nz

    def on_device(near_tiles, near_side, skeleton, far_coupling, far_basis, sources):
        rows, tile = sources.shape[2] * sources.shape[3], sources.shape[4]
        rank = skeleton.shape[2]
        any_space = pl.BlockSpec(memory_space=pl.ANY)
        vmem = pl.BlockSpec(memory_space=pltpu.VMEM)
        dma = pltpu.SemaphoreType.DMA
        result = pl.pallas_call(
            functools.partial(kernel, (ns, nt, nx, nz)),
            out_shape=jax.ShapeDtypeStruct((2, rows, tile), F32),
            in_specs=[any_space, vmem, vmem, any_space, any_space, any_space],
            out_specs=vmem,
            scratch_shapes=[
                pltpu.VMEM((2, 2, tile, tile), F32),
                pltpu.VMEM((2, 2, tile, tile), BF16),
                pltpu.VMEM((2, 2, tile, tile), BF16),
                pltpu.VMEM((2, rank, nt * rank), F32),
                pltpu.VMEM((2, rank, tile), F32),
                pltpu.VMEM((4 * rank, 2 * tile), BF16),
                pltpu.VMEM((2, rows, tile), F32),
                pltpu.VMEM((8, 2 * rank), jnp.int32),
                pltpu.VMEM((8, 2 * rank), jnp.int32),
                pltpu.VMEM((tile, 2 * rank), BF16),
                pltpu.VMEM((nz, nx * 2 * rank, 4 * rank), BF16),
                pltpu.VMEM((nz, nx * 2 * rank, 4 * rank), BF16),
                pltpu.VMEM((3, 2, rows, tile), F32),
                pltpu.VMEM((2, rows, tile), F32),
                pltpu.VMEM((nz, nx, rows, 2 * rank), F32),
                pltpu.VMEM((rows, 2 * rank), F32),
                pltpu.VMEM((nt - 1, 1, 128), F32),
                pltpu.VMEM((1, 128), F32),
                dma((7,)),
                dma((2,)),
                dma((3,)),
                dma((3,)),
                dma,
                dma((nz,)),
                dma,
                dma,
            ],
            compiler_params=pltpu.CompilerParams(collective_id=0, has_side_effects=True),
        )(
            near_tiles[0],
            near_side,
            skeleton[0],
            far_coupling[0],
            far_basis[0],
            sources[0].reshape(2, rows, tile),
        )
        return result.reshape(sources.shape)

    placed = (
        P("slab", None, None, None, "trace"),
        P("slab", "trace"),
        P("slab", "trace", None),
        P("slab", None, "trace", None),
        P("slab", None, None, "trace"),
        P("slab", None, None, None, "trace"),
    )
    return jax.shard_map(
        on_device,
        mesh=mesh,
        in_specs=placed,
        out_specs=P("slab", None, None, None, "trace"),
        check_vma=False,
    )
```

```python
import functools

import jax
import jax.numpy as jnp
from jax import lax
from jax.experimental import pallas as pl
from jax.experimental.pallas import tpu as pltpu
from jax.sharding import PartitionSpec as P

MESH = pl.DeviceIdType.MESH
F32 = jnp.float32
BF16 = jnp.bfloat16
small_eps = 1e-06


def halves(x):
    hi = x.astype(BF16)
    lo = (x - hi.astype(F32)).astype(BF16)
    return hi, lo


def thirds(x):
    hi = x.astype(BF16)
    rest = x - hi.astype(F32)
    mid = rest.astype(BF16)
    lo = (rest - mid.astype(F32)).astype(BF16)
    return hi, mid, lo


def mm(a, b):
    return jnp.dot(a, b, preferred_element_type=F32)


def outward(k, n):
    return (n // 2 + ((k + 1) // 2) * (1 - 2 * (k % 2))) % n


def joined(x):
    hi = x.astype(BF16).astype(F32)
    return jnp.concatenate([hi, x - hi], axis=0).astype(BF16)


def kernel(
    sizes,
    near_hbm,
    side_ref,
    skel_ref,
    coup_hbm,
    basis_hbm,
    src_hbm,
    u_hbm,
    scale_ref,
    near_f,
    near_hi,
    near_lo,
    coup_f,
    basis_f,
    basis_in,
    basis_w,
    src_v,
    skel_out,
    skel_next,
    pick_w,
    wp,
    wc,
    n_in,
    n_out,
    c_in,
    c_out,
    p_in,
    p_out,
    e_in,
    e_out,
    u_v,
    w_sem,
    skel_sem,
    b_send,
    b_recv,
    n_send,
    n_recv,
    c_send,
    c_recv,
    p_send,
    p_recv,
    e_send,
    e_recv,
):
    ns, nt, nx, nz = sizes
    tile = src_v.shape[2]
    rows = src_v.shape[1]
    rank = skel_ref.shape[1]
    n = 2 * rank
    half = rows // 2
    slab = lax.axis_index("slab")
    me = lax.axis_index("trace")
    my_x, my_z = me // nz, me % nz
    has_next = slab < ns - 1
    has_prev = slab > 0
    from_far = slab > 1
    first = lax.broadcasted_iota(jnp.int32, (rank, n), 1) < rank

    basis_load = pltpu.make_async_copy(basis_hbm, basis_f, w_sem.at[0])
    coup_load = pltpu.make_async_copy(coup_hbm, coup_f, w_sem.at[1])
    src_load = pltpu.make_async_copy(src_hbm, src_v, w_sem.at[2])
    near_loads = [
        pltpu.make_async_copy(
            near_hbm.at[slot, part], near_f.at[slot, part], w_sem.at[3 + 2 * slot + part]
        )
        for slot in range(2)
        for part in range(2)
    ]
    for load in [src_load, coup_load, basis_load] + near_loads:
        load.start()

    spread = [
        (int(outward(k // nx, nz)), int(outward(k % nx, nx))) for k in range(nt)
    ]
    wrap_x = [lax.rem(my_x + dx, nx) * nz for dx in range(nx)]
    wrap_z = [lax.rem(my_z + dz, nz) for dz in range(nz)]

    def block_at(dz, dx):
        return wrap_x[dx] + wrap_z[dz]

    barrier = pltpu.get_barrier_semaphore()

    def greet(s, t):
        pl.semaphore_signal(barrier, inc=1, device_id=(s, t), device_id_type=MESH)

    @pl.when(has_prev)
    def _():
        for dz, dx in spread:
            greet(slab - 1, block_at(dz, dx))

    for dz, dx in spread[:-1]:
        greet(slab, block_at(dz, dx))

    @pl.when(has_next)
    def _():
        greet(slab + 1, me)

    twin = jnp.concatenate([skel_ref[...], skel_ref[...]], axis=1)
    skel_out[...] = jnp.broadcast_to(twin, skel_out.shape)
    side = side_ref[...]

    def choose(right, left):
        return jnp.where(jnp.broadcast_to(side, left.shape) > 0, right, left)

    def set_basis(i, b_re, b_im):
        top = jnp.concatenate([b_re, -b_im], axis=0)
        bottom = jnp.concatenate([b_im, b_re], axis=0)
        for j, m in enumerate((top, bottom)):
            hi, lo = halves(m)
            basis_w[i, :n, j * tile : (j + 1) * tile] = hi
            basis_w[i, n:, j * tile : (j + 1) * tile] = lo

    def far_part(i, coef):
        hi, lo = halves(coef)
        lhs = jnp.concatenate(
            [jnp.concatenate([hi, hi], axis=1), jnp.concatenate([lo, lo], axis=1)], axis=0
        )
        far = mm(lhs, basis_w[i])
        far = far[:rows] + far[rows:]
        return far[:, :tile], far[:, tile:]

    coup_load.wait()
    place = lax.broadcasted_iota(jnp.int32, (n, n), 1)

    @pl.loop(0, nt // 2, unroll=min(4, nt // 2))
    def _(t):
        at = pl.ds(pl.multiple_of(t * n, n), n)
        a = jnp.concatenate([coup_f[0, :, at], coup_f[1, :, at]], axis=0).T
        b = pltpu.roll(jnp.where(place < rank, a, -a), rank, 1)
        for odd in range(2):
            c = 2 * t + odd
            keep = jnp.logical_and(side + me != c, me != c).astype(F32)
            cx, cz = c // nz, c % nz
            for i, m in enumerate((a, b)):
                hi, lo = halves(m[odd * rank : (odd + 1) * rank] * keep)
                out_at = pl.ds(pl.multiple_of(cx * n + i * rank, rank), rank)
                wc[cz, out_at, :n] = hi
                wc[cz, out_at, n:] = lo

    basis_load.wait()
    set_basis(0, basis_f[0], basis_f[1])
    src_load.wait()

    pl.semaphore_wait(
        barrier, nt - 1 + nt * has_next.astype(jnp.int32) + has_prev.astype(jnp.int32)
    )

    skel_copy = pltpu.make_async_remote_copy(
        src_ref=skel_out,
        dst_ref=skel_next,
        send_sem=skel_sem.at[0],
        recv_sem=skel_sem.at[1],
        device_id=(slab - 1, me),
        device_id_type=MESH,
    )

    @pl.when(has_prev)
    def _():
        skel_copy.start()

    def send_three(src, dst, send, recv):
        for i, shift in enumerate((nt - 1, 1, 0)):
            pltpu.make_async_remote_copy(
                src_ref=src,
                dst_ref=dst.at[i],
                send_sem=send.at[i],
                recv_sem=recv.at[i],
                device_id=(slab + 1, (me + shift) % nt),
                device_id_type=MESH,
            ).start()

    def send_p(stream):
        for dz, dx in spread:
            pltpu.make_async_remote_copy(
                src_ref=p_out.at[stream],
                dst_ref=p_in.at[stream, dz, my_x],
                send_sem=p_send.at[stream],
                recv_sem=p_recv.at[stream, dz],
                device_id=(slab + 1, block_at(dz, dx)),
                device_id_type=MESH,
            ).start()

    def pick(x):
        parts = mm(jnp.concatenate(thirds(x), axis=0), pick_w[...])
        m = 2 * rows
        got = parts[:m] + parts[m : 2 * m] + parts[2 * m :]
        return jnp.where(first[:rows], got[:rows], got[rows:])

    @pl.when(slab == 0)
    def _():
        send_three(src_v, n_in, n_send, n_recv)
        n_in[...] = jnp.zeros_like(n_in)
        p_in[...] = jnp.zeros_like(p_in)

    @pl.when(jnp.logical_and(has_prev, has_next))
    def _():
        send_three(basis_f, basis_in, b_send, b_recv)

    @pl.when(has_next)
    def _():
        skel_copy.wait_recv()
        unknown = lax.broadcasted_iota(jnp.int32, (tile, n), 0)
        pick_w[...] = (unknown == skel_next[:1, :]).astype(BF16)

    @pl.when(jnp.logical_not(has_next))
    def _():
        pick_w[...] = jnp.zeros_like(pick_w)

    @pl.when(slab == 0)
    def _():
        p_first = pick(src_v[...].reshape(2 * rows, tile))
        for stream in range(2):
            p_out[stream] = p_first[stream * half : (stream + 1) * half]
            send_p(stream)

    for slot in range(2):
        for part in range(2):
            near_loads[2 * slot + part].wait()

            @pl.loop(0, tile // 32)
            def _(i):
                at = pl.ds(pl.multiple_of(i * 32, 32), 32)
                hi, lo = halves(near_f[slot, part, at, :])
                near_hi[slot, part, at, :] = hi
                near_lo[slot, part, at, :] = lo

    b_all = basis_f[...].reshape(n, tile)
    picked = mm(jnp.concatenate(thirds(b_all), axis=0), pick_w[...])
    picked = picked[:n] + picked[n : 2 * n] + picked[2 * n :]
    s_re, s_im = picked[:rank], picked[rank:]
    s_mat = jnp.concatenate([jnp.where(first, s_re, s_im), jnp.where(first, -s_im, s_re)], axis=0)
    s_w = jnp.concatenate(halves(s_mat), axis=1)
    s_w = jnp.concatenate([s_w, s_w], axis=0)

    @pl.loop(0, nz, unroll=2)
    def _(z):
        prod = mm(wc[z], s_w)
        hi, lo = halves(prod[:, :n] + prod[:, n:])
        wp[z, :, :n] = hi
        wp[z, :, n:] = lo

    def near(slot, x, m):
        hi, lo = halves(x)
        both = jnp.concatenate([hi, lo], axis=0)
        sums = []
        for part in range(2):
            prod = mm(both, near_hi[slot, part])
            sums.append(prod[: 2 * m] + prod[2 * m :] + mm(hi, near_lo[slot, part]))
        return sums[0][:m] - sums[1][m:], sums[1][:m] + sums[0][m:]

    @pl.when(from_far)
    def _():
        for i in range(3):
            pltpu.make_async_copy(basis_in.at[i], basis_in.at[i], b_recv.at[i]).wait()
        set_basis(1, *near(0, basis_in[2].reshape(n, tile), rank))
        beside = jnp.where(
            jnp.broadcast_to(side, (n, tile)) > 0,
            basis_in[0].reshape(n, tile),
            basis_in[1].reshape(n, tile),
        )
        set_basis(2, *near(1, beside, rank))

    @pl.when(has_prev)
    def _():
        for i in range(3):
            pltpu.make_async_copy(n_in.at[i], n_in.at[i], n_recv.at[i]).wait()

    own_re, own_im = near(0, n_in[2].reshape(2 * rows, tile), rows)
    next_re, next_im = near(1, choose(n_in[0], n_in[1]).reshape(2 * rows, tile), rows)
    n_out[0] = own_re + next_re + src_v[0]
    n_out[1] = own_im + next_im + src_v[1]

    order = [int(outward(k, nz)) for k in range(nz)][::-1]
    early = order[: nz // 2 + 1]
    late = order[nz // 2 + 1 :]

    def wait_p(stream, group):
        @pl.when(has_prev)
        def _():
            for dz in group:
                pltpu.make_async_copy(
                    p_in.at[stream, dz], p_in.at[stream, dz], p_recv.at[stream, dz]
                ).wait()

    def p_lhs(stream, dz):
        return joined(jnp.concatenate([p_in[stream, dz, x] for x in range(nx)], axis=1))

    def times(w, stream, group):
        total = None
        for dz in group:
            term = mm(p_lhs(stream, dz), w[(my_z - dz + nz) % nz])
            total = term if total is None else total + term
        return total

    def fold(acc):
        acc = acc[:half] + acc[half:]
        return acc[:, :n] + acc[:, n:]

    wait_p(0, early)
    p_acc = times(wp, 0, early)
    c_acc = times(wc, 0, early)

    @pl.when(from_far)
    def _():
        for i in range(3):
            pltpu.make_async_copy(c_in.at[i], c_in.at[i], c_recv.at[i]).wait()
        f_re, f_im = far_part(1, c_in[2])
        g_re, g_im = far_part(2, choose(c_in[0], c_in[1]))
        n_out[0] += f_re + g_re
        n_out[1] += f_im + g_im

    @pl.when(jnp.logical_and(has_prev, has_next))
    def _():
        send_three(n_out, n_in, n_send, n_recv)

    n_re, n_im = n_out[0], n_out[1]
    ahead = pick(jnp.concatenate([n_re, n_im], axis=0))

    coefs = []
    for stream in range(2):
        if stream == 1:
            wait_p(1, early)
            p_acc = times(wp, 1, early)
            c_acc = times(wc, 1, early)
        wait_p(stream, late)
        p_new = ahead[stream * half : (stream + 1) * half] + fold(p_acc + times(wp, stream, late))
        if stream == 1:
            coefs.append(fold(c_acc + times(wc, stream, late)))

        @pl.when(jnp.logical_and(has_prev, has_next))
        def _():
            p_out[stream] = p_new
            if stream == 1:
                c_out[...] = jnp.concatenate(coefs, axis=0)
                send_three(c_out, c_in, c_send, c_recv)
            send_p(stream)

        if stream == 0:
            coefs.append(fold(c_acc + times(wc, stream, late)))
    coef = jnp.concatenate(coefs, axis=0)

    f_re, f_im = far_part(0, coef)
    u_re = n_re + f_re
    u_im = n_im + f_im

    part_sum = jnp.sum(u_re * u_re + u_im * u_im, axis=1, keepdims=True)
    diag = (
        lax.broadcasted_iota(jnp.int32, (rows, 128), 0)
        == lax.broadcasted_iota(jnp.int32, (rows, 128), 1)
    ).astype(F32)
    e_out[...] = jnp.sum(part_sum * diag, axis=0, keepdims=True)

    for k, (dz, dx) in enumerate(spread[:-1]):
        pltpu.make_async_remote_copy(
            src_ref=e_out,
            dst_ref=e_in.at[k],
            send_sem=e_send,
            recv_sem=e_recv,
            device_id=(slab, block_at(dz, dx)),
            device_id_type=MESH,
        ).start()

    u_v[0] = u_re
    u_v[1] = u_im
    u_store = pltpu.make_async_copy(u_v, u_hbm, w_sem.at[7])
    u_store.start()

    pltpu.make_async_copy(e_in, e_in, e_recv).wait()
    total = e_out[...] + jnp.sum(e_in[...], axis=0)
    energy = jnp.sum(total * diag, axis=1, keepdims=True) / (2 * tile * nt)
    scale_ref[...] = jnp.broadcast_to(1.0 / jnp.sqrt(energy + small_eps), scale_ref.shape)

    u_store.wait()
    pltpu.make_async_copy(e_in, e_in, e_send).wait()

    @pl.when(has_next)
    def _():
        for i in range(3):
            pltpu.make_async_copy(n_out, n_out, n_send.at[i]).wait()
        for stream in range(2):
            pltpu.make_async_copy(p_in.at[stream], p_in.at[stream], p_send.at[stream]).wait()

    @pl.when(jnp.logical_and(has_prev, has_next))
    def _():
        for i in range(3):
            pltpu.make_async_copy(basis_f, basis_f, b_send.at[i]).wait()
            pltpu.make_async_copy(c_out, c_out, c_send.at[i]).wait()

    @pl.when(has_prev)
    def _():
        skel_copy.wait_send()


def solution(mesh):
    ns, nt = mesh.shape["slab"], mesh.shape["trace"]
    nz = 8 if nt % 8 == 0 else nt
    nx = nt // nz

    def on_device(near_tiles, near_side, skeleton, far_coupling, far_basis, sources):
        rows, tile = sources.shape[2] * sources.shape[3], sources.shape[4]
        rank = skeleton.shape[2]
        any_space = pl.BlockSpec(memory_space=pl.ANY)
        vmem = pl.BlockSpec(memory_space=pltpu.VMEM)
        dma = pltpu.SemaphoreType.DMA
        u, scale = pl.pallas_call(
            functools.partial(kernel, (ns, nt, nx, nz)),
            out_shape=(
                jax.ShapeDtypeStruct((2, rows, tile), F32),
                jax.ShapeDtypeStruct((rows, tile), F32),
            ),
            in_specs=[any_space, vmem, vmem, any_space, any_space, any_space],
            out_specs=(any_space, vmem),
            scratch_shapes=[
                pltpu.VMEM((2, 2, tile, tile), F32),
                pltpu.VMEM((2, 2, tile, tile), BF16),
                pltpu.VMEM((2, 2, tile, tile), BF16),
                pltpu.VMEM((2, rank, nt * rank), F32),
                pltpu.VMEM((2, rank, tile), F32),
                pltpu.VMEM((3, 2, rank, tile), F32),
                pltpu.VMEM((3, 4 * rank, 2 * tile), BF16),
                pltpu.VMEM((2, rows, tile), F32),
                pltpu.VMEM((8, 2 * rank), jnp.int32),
                pltpu.VMEM((8, 2 * rank), jnp.int32),
                pltpu.VMEM((tile, 2 * rank), BF16),
                pltpu.VMEM((nz, nx * 2 * rank, 4 * rank), BF16),
                pltpu.VMEM((nz, nx * 2 * rank, 4 * rank), BF16),
                pltpu.VMEM((3, 2, rows, tile), F32),
                pltpu.VMEM((2, rows, tile), F32),
                pltpu.VMEM((3, rows, 2 * rank), F32),
                pltpu.VMEM((rows, 2 * rank), F32),
                pltpu.VMEM((2, nz, nx, rows // 2, 2 * rank), F32),
                pltpu.VMEM((2, rows // 2, 2 * rank), F32),
                pltpu.VMEM((nt - 1, 1, 128), F32),
                pltpu.VMEM((1, 128), F32),
                pltpu.VMEM((2, rows, tile), F32),
                dma((8,)),
                dma((2,)),
                dma((3,)),
                dma((3,)),
                dma((3,)),
                dma((3,)),
                dma((3,)),
                dma((3,)),
                dma((2,)),
                dma((2, nz)),
                dma,
                dma,
            ],
            compiler_params=pltpu.CompilerParams(collective_id=0, has_side_effects=True),
        )(
            near_tiles[0],
            near_side,
            skeleton[0],
            far_coupling[0],
            far_basis[0],
            sources[0].reshape(2, rows, tile),
        )
        return (u * scale[None]).reshape(sources.shape)

    placed = (
        P("slab", None, None, None, "trace"),
        P("slab", "trace"),
        P("slab", "trace", None),
        P("slab", None, "trace", None),
        P("slab", None, None, "trace"),
        P("slab", None, None, None, "trace"),
    )
    return jax.shard_map(
        on_device,
        mesh=mesh,
        in_specs=placed,
        out_specs=P("slab", None, None, None, "trace"),
        check_vma=False,
    )
```

```python
import functools

import jax
import jax.numpy as jnp
from jax import lax
from jax.experimental import pallas as pl
from jax.experimental.pallas import tpu as pltpu
from jax.sharding import PartitionSpec as P

MESH = pl.DeviceIdType.MESH
F32 = jnp.float32
BF16 = jnp.bfloat16
small_eps = 1e-06


def halves(x):
    hi = x.astype(BF16)
    lo = (x - hi.astype(F32)).astype(BF16)
    return hi, lo


def thirds(x):
    hi = x.astype(BF16)
    rest = x - hi.astype(F32)
    mid = rest.astype(BF16)
    lo = (rest - mid.astype(F32)).astype(BF16)
    return hi, mid, lo


def mm(a, b):
    return jnp.dot(a, b, preferred_element_type=F32)


def outward(k, n):
    return (n // 2 + ((k + 1) // 2) * (1 - 2 * (k % 2))) % n


def joined(x):
    hi = x.astype(BF16).astype(F32)
    return jnp.concatenate([hi, x - hi], axis=0).astype(BF16)


def kernel(
    sizes,
    near_hbm,
    side_ref,
    skel_ref,
    coup_hbm,
    basis_hbm,
    src_hbm,
    u_hbm,
    scale_ref,
    near_f,
    near_hi,
    near_lo,
    coup_f,
    basis_f,
    basis_w,
    nsel,
    a_v,
    acc_v,
    src_v,
    skel_out,
    skel_next,
    pick_w,
    wp,
    wc,
    u_in,
    u_out,
    n_v,
    p_in,
    p_out,
    e_in,
    e_out,
    w_sem,
    skel_sem,
    u_send,
    u_recv,
    p_send,
    p_recv,
    e_send,
    e_recv,
):
    ns, nt, nx, nz = sizes
    tile = src_v.shape[2]
    rows = src_v.shape[1]
    rank = skel_ref.shape[1]
    n = 2 * rank
    half = rows // 2
    slab = lax.axis_index("slab")
    me = lax.axis_index("trace")
    my_x, my_z = me // nz, me % nz
    has_next = slab < ns - 1
    has_prev = slab > 0
    from_far = slab > 1
    first = lax.broadcasted_iota(jnp.int32, (rank, n), 1) < rank

    basis_load = pltpu.make_async_copy(basis_hbm, basis_f, w_sem.at[0])
    coup_load = pltpu.make_async_copy(coup_hbm, coup_f, w_sem.at[1])
    src_load = pltpu.make_async_copy(src_hbm, src_v, w_sem.at[2])
    near_loads = [
        pltpu.make_async_copy(
            near_hbm.at[slot, part], near_f.at[slot, part], w_sem.at[3 + 2 * slot + part]
        )
        for slot in range(2)
        for part in range(2)
    ]
    for load in [src_load, coup_load, basis_load] + near_loads:
        load.start()

    spread = [
        (int(outward(k // nx, nz)), int(outward(k % nx, nx))) for k in range(nt)
    ]
    wrap_x = [lax.rem(my_x + dx, nx) * nz for dx in range(nx)]
    wrap_z = [lax.rem(my_z + dz, nz) for dz in range(nz)]

    def block_at(dz, dx):
        return wrap_x[dx] + wrap_z[dz]

    barrier = pltpu.get_barrier_semaphore()

    def greet(s, t):
        pl.semaphore_signal(barrier, inc=1, device_id=(s, t), device_id_type=MESH)

    @pl.when(has_prev)
    def _():
        for dz, dx in spread:
            greet(slab - 1, block_at(dz, dx))

    for dz, dx in spread[:-1]:
        greet(slab, block_at(dz, dx))

    @pl.when(has_next)
    def _():
        greet(slab + 1, me)

    twin = jnp.concatenate([skel_ref[...], skel_ref[...]], axis=1)
    skel_out[...] = jnp.broadcast_to(twin, skel_out.shape)
    side = side_ref[...]

    def choose(right, left):
        return jnp.where(jnp.broadcast_to(side, left.shape) > 0, right, left)

    def set_basis(b_re, b_im):
        top = jnp.concatenate([b_re, -b_im], axis=0)
        bottom = jnp.concatenate([b_im, b_re], axis=0)
        for j, m in enumerate((top, bottom)):
            hi, lo = halves(m)
            basis_w[:n, j * tile : (j + 1) * tile] = hi
            basis_w[n:, j * tile : (j + 1) * tile] = lo

    def far_part(coef):
        hi, lo = halves(coef)
        lhs = jnp.concatenate(
            [jnp.concatenate([hi, hi], axis=1), jnp.concatenate([lo, lo], axis=1)], axis=0
        )
        far = mm(lhs, basis_w[...])
        far = far[:rows] + far[rows:]
        return far[:, :tile], far[:, tile:]

    coup_load.wait()
    place = lax.broadcasted_iota(jnp.int32, (n, n), 1)

    @pl.loop(0, nt // 2, unroll=min(4, nt // 2))
    def _(t):
        at = pl.ds(pl.multiple_of(t * n, n), n)
        a = jnp.concatenate([coup_f[0, :, at], coup_f[1, :, at]], axis=0).T
        b = pltpu.roll(jnp.where(place < rank, a, -a), rank, 1)
        for odd in range(2):
            c = 2 * t + odd
            keep = jnp.logical_and(side + me != c, me != c).astype(F32)
            cx, cz = c // nz, c % nz
            for i, m in enumerate((a, b)):
                hi, lo = halves(m[odd * rank : (odd + 1) * rank] * keep)
                out_at = pl.ds(pl.multiple_of(cx * n + i * rank, rank), rank)
                wc[cz, out_at, :n] = hi
                wc[cz, out_at, n:] = lo

    basis_load.wait()
    set_basis(basis_f[0], basis_f[1])
    src_load.wait()

    pl.semaphore_wait(
        barrier, nt - 1 + nt * has_next.astype(jnp.int32) + has_prev.astype(jnp.int32)
    )

    skel_copy = pltpu.make_async_remote_copy(
        src_ref=skel_out,
        dst_ref=skel_next,
        send_sem=skel_sem.at[0],
        recv_sem=skel_sem.at[1],
        device_id=(slab - 1, me),
        device_id_type=MESH,
    )

    @pl.when(has_prev)
    def _():
        skel_copy.start()

    def send_three(src, dst, send, recv):
        for i, shift in enumerate((nt - 1, 1, 0)):
            pltpu.make_async_remote_copy(
                src_ref=src,
                dst_ref=dst.at[i],
                send_sem=send.at[i],
                recv_sem=recv.at[i],
                device_id=(slab + 1, (me + shift) % nt),
                device_id_type=MESH,
            ).start()

    def send_p(stream):
        for dz, dx in spread:
            pltpu.make_async_remote_copy(
                src_ref=p_out.at[stream],
                dst_ref=p_in.at[stream, dz, my_x],
                send_sem=p_send.at[stream],
                recv_sem=p_recv.at[stream, dz],
                device_id=(slab + 1, block_at(dz, dx)),
                device_id_type=MESH,
            ).start()

    def pick(x):
        parts = mm(jnp.concatenate(thirds(x), axis=0), pick_w[...])
        m = 2 * rows
        got = parts[:m] + parts[m : 2 * m] + parts[2 * m :]
        return jnp.where(first[:rows], got[:rows], got[rows:])

    @pl.when(slab == 0)
    def _():
        send_three(src_v, u_in, u_send, u_recv)
        u_in[...] = jnp.zeros_like(u_in)
        p_in[...] = jnp.zeros_like(p_in)

    @pl.when(has_next)
    def _():
        skel_copy.wait_recv()
        unknown = lax.broadcasted_iota(jnp.int32, (tile, n), 0)
        pick_w[...] = (unknown == skel_next[:1, :]).astype(BF16)

    @pl.when(jnp.logical_not(has_next))
    def _():
        pick_w[...] = jnp.zeros_like(pick_w)

    @pl.when(slab == 0)
    def _():
        p_first = pick(src_v[...].reshape(2 * rows, tile))
        for stream in range(2):
            p_out[stream] = p_first[stream * half : (stream + 1) * half]
            send_p(stream)

    for slot in range(2):
        for part in range(2):
            near_loads[2 * slot + part].wait()

            @pl.loop(0, tile // 32)
            def _(i):
                at = pl.ds(pl.multiple_of(i * 32, 32), 32)
                hi, lo = halves(near_f[slot, part, at, :])
                near_hi[slot, part, at, :] = hi
                near_lo[slot, part, at, :] = lo

    b_all = basis_f[...].reshape(n, tile)
    picked = mm(jnp.concatenate(thirds(b_all), axis=0), pick_w[...])
    picked = picked[:n] + picked[n : 2 * n] + picked[2 * n :]
    s_re, s_im = picked[:rank], picked[rank:]
    s_mat = jnp.concatenate([jnp.where(first, s_re, s_im), jnp.where(first, -s_im, s_re)], axis=0)
    s_w = jnp.concatenate(halves(s_mat), axis=1)
    s_w = jnp.concatenate([s_w, s_w], axis=0)

    @pl.loop(0, nz, unroll=2)
    def _(z):
        prod = mm(wc[z], s_w)
        hi, lo = halves(prod[:, :n] + prod[:, n:])
        wp[z, :, :n] = hi
        wp[z, :, n:] = lo

    @pl.when(from_far)
    def _():
        in_first = lax.broadcasted_iota(jnp.int32, (tile, n), 1) < rank
        for slot in range(2):
            for i, w in enumerate((near_hi, near_lo)):
                re, im = mm(w[slot, 0], pick_w[...]), mm(w[slot, 1], pick_w[...])
                nsel[slot, :, i * n : (i + 1) * n] = jnp.where(in_first, re, im).astype(BF16)
        a_v[...] = pick(src_v[...].reshape(2 * rows, tile))

    def wait_u():
        for i in range(3):
            pltpu.make_async_copy(u_in.at[i], u_in.at[i], u_recv.at[i]).wait()

    def incoming(slot):
        x = u_in[2] if slot == 0 else choose(u_in[0], u_in[1])
        return halves(x.reshape(2 * rows, tile))

    def near():
        sums = [None, None]
        for slot in range(2):
            hi, lo = incoming(slot)
            both = jnp.concatenate([hi, lo], axis=0)
            for part in range(2):
                prod = mm(both, near_hi[slot, part])
                term = prod[: 2 * rows] + prod[2 * rows :] + mm(hi, near_lo[slot, part])
                sums[part] = term if slot == 0 else sums[part] + term
        n_v[0] = sums[0][:rows] - sums[1][rows:] + src_v[0]
        n_v[1] = sums[1][:rows] + sums[0][rows:] + src_v[1]

    @pl.when(jnp.logical_not(from_far))
    def _():
        @pl.when(has_prev)
        def _():
            wait_u()

        near()
        a_v[...] = pick(n_v[...].reshape(2 * rows, tile))

    order = [int(outward(k, nz)) for k in range(nz)][::-1]
    early = order[: nz // 2 + 1]
    late = order[nz // 2 + 1 :]

    def wait_p(stream, group):
        @pl.when(has_prev)
        def _():
            for dz in group:
                pltpu.make_async_copy(
                    p_in.at[stream, dz], p_in.at[stream, dz], p_recv.at[stream, dz]
                ).wait()

    def p_lhs(stream, dz):
        return joined(jnp.concatenate([p_in[stream, dz, x] for x in range(nx)], axis=1))

    def times(w, stream, group):
        total = None
        for dz in group:
            term = mm(p_lhs(stream, dz), w[(my_z - dz + nz) % nz])
            total = term if total is None else total + term
        return total

    def fold(acc):
        acc = acc[:half] + acc[half:]
        return acc[:, :n] + acc[:, n:]

    sends_on = jnp.logical_and(has_prev, has_next)

    def first_part(stream):
        wait_p(stream, early)

        @pl.when(sends_on)
        def _():
            acc_v[...] = times(wp, stream, early)

    def last_part(stream):
        @pl.when(sends_on)
        def _():
            p_out[stream] = a_v[stream * half : (stream + 1) * half] + fold(
                acc_v[...] + times(wp, stream, late)
            )
            send_p(stream)

    first_part(0)
    c_first = times(wc, 0, early)

    @pl.when(from_far)
    def _():
        wait_u()

        @pl.when(has_next)
        def _():
            total = None
            for slot in range(2):
                term = mm(jnp.concatenate(incoming(slot), axis=0), nsel[slot])
                total = term if total is None else total + term
            total = total[: 2 * rows] + total[2 * rows :]
            total = total[:, :n] + total[:, n:]
            turned = pltpu.roll(total[rows:], rank, 1)
            a_v[...] += total[:rows] + jnp.where(first[:rows], -turned, turned)

    wait_p(0, late)
    last_part(0)
    first_part(1)
    wait_p(1, late)
    last_part(1)

    @pl.when(from_far)
    def _():
        near()

    coef = jnp.concatenate(
        [fold(c_first + times(wc, 0, late)), fold(times(wc, 1, order))], axis=0
    )
    f_re, f_im = far_part(coef)
    u_re = n_v[0] + f_re
    u_im = n_v[1] + f_im
    u_out[0] = u_re
    u_out[1] = u_im

    @pl.when(sends_on)
    def _():
        send_three(u_out, u_in, u_send, u_recv)

    part_sum = jnp.sum(u_re * u_re + u_im * u_im, axis=1, keepdims=True)
    diag = (
        lax.broadcasted_iota(jnp.int32, (rows, 128), 0)
        == lax.broadcasted_iota(jnp.int32, (rows, 128), 1)
    ).astype(F32)
    e_out[...] = jnp.sum(part_sum * diag, axis=0, keepdims=True)

    for k, (dz, dx) in enumerate(spread[:-1]):
        pltpu.make_async_remote_copy(
            src_ref=e_out,
            dst_ref=e_in.at[k],
            send_sem=e_send,
            recv_sem=e_recv,
            device_id=(slab, block_at(dz, dx)),
            device_id_type=MESH,
        ).start()

    u_store = pltpu.make_async_copy(u_out, u_hbm, w_sem.at[7])
    u_store.start()

    pltpu.make_async_copy(e_in, e_in, e_recv).wait()
    total = e_out[...] + jnp.sum(e_in[...], axis=0)
    energy = jnp.sum(total * diag, axis=1, keepdims=True) / (2 * tile * nt)
    scale_ref[...] = jnp.broadcast_to(1.0 / jnp.sqrt(energy + small_eps), scale_ref.shape)

    u_store.wait()
    pltpu.make_async_copy(e_in, e_in, e_send).wait()

    @pl.when(has_next)
    def _():
        for i in range(3):
            pltpu.make_async_copy(u_out, u_out, u_send.at[i]).wait()
        for stream in range(2):
            pltpu.make_async_copy(p_in.at[stream], p_in.at[stream], p_send.at[stream]).wait()

    @pl.when(has_prev)
    def _():
        skel_copy.wait_send()


def solution(mesh):
    ns, nt = mesh.shape["slab"], mesh.shape["trace"]
    nz = 8 if nt % 8 == 0 else nt
    nx = nt // nz

    def on_device(near_tiles, near_side, skeleton, far_coupling, far_basis, sources):
        rows, tile = sources.shape[2] * sources.shape[3], sources.shape[4]
        rank = skeleton.shape[2]
        any_space = pl.BlockSpec(memory_space=pl.ANY)
        vmem = pl.BlockSpec(memory_space=pltpu.VMEM)
        dma = pltpu.SemaphoreType.DMA
        u, scale = pl.pallas_call(
            functools.partial(kernel, (ns, nt, nx, nz)),
            out_shape=(
                jax.ShapeDtypeStruct((2, rows, tile), F32),
                jax.ShapeDtypeStruct((rows, tile), F32),
            ),
            in_specs=[any_space, vmem, vmem, any_space, any_space, any_space],
            out_specs=(any_space, vmem),
            scratch_shapes=[
                pltpu.VMEM((2, 2, tile, tile), F32),
                pltpu.VMEM((2, 2, tile, tile), BF16),
                pltpu.VMEM((2, 2, tile, tile), BF16),
                pltpu.VMEM((2, rank, nt * rank), F32),
                pltpu.VMEM((2, rank, tile), F32),
                pltpu.VMEM((4 * rank, 2 * tile), BF16),
                pltpu.VMEM((2, tile, 4 * rank), BF16),
                pltpu.VMEM((rows, 2 * rank), F32),
                pltpu.VMEM((rows, 4 * rank), F32),
                pltpu.VMEM((2, rows, tile), F32),
                pltpu.VMEM((8, 2 * rank), jnp.int32),
                pltpu.VMEM((8, 2 * rank), jnp.int32),
                pltpu.VMEM((tile, 2 * rank), BF16),
                pltpu.VMEM((nz, nx * 2 * rank, 4 * rank), BF16),
                pltpu.VMEM((nz, nx * 2 * rank, 4 * rank), BF16),
                pltpu.VMEM((3, 2, rows, tile), F32),
                pltpu.VMEM((2, rows, tile), F32),
                pltpu.VMEM((2, rows, tile), F32),
                pltpu.VMEM((2, nz, nx, rows // 2, 2 * rank), F32),
                pltpu.VMEM((2, rows // 2, 2 * rank), F32),
                pltpu.VMEM((nt - 1, 1, 128), F32),
                pltpu.VMEM((1, 128), F32),
                dma((8,)),
                dma((2,)),
                dma((3,)),
                dma((3,)),
                dma((2,)),
                dma((2, nz)),
                dma,
                dma,
            ],
            compiler_params=pltpu.CompilerParams(collective_id=0, has_side_effects=True),
        )(
            near_tiles[0],
            near_side,
            skeleton[0],
            far_coupling[0],
            far_basis[0],
            sources[0].reshape(2, rows, tile),
        )
        return (u * scale[None]).reshape(sources.shape)

    placed = (
        P("slab", None, None, None, "trace"),
        P("slab", "trace"),
        P("slab", "trace", None),
        P("slab", None, "trace", None),
        P("slab", None, None, "trace"),
        P("slab", None, None, None, "trace"),
    )
    return jax.shard_map(
        on_device,
        mesh=mesh,
        in_specs=placed,
        out_specs=P("slab", None, None, None, "trace"),
        check_vma=False,
    )
```

```python
import functools

import jax
import jax.numpy as jnp
from jax import lax
from jax.experimental import pallas as pl
from jax.experimental.pallas import tpu as pltpu
from jax.sharding import PartitionSpec as P

MESH = pl.DeviceIdType.MESH
F32 = jnp.float32
BF16 = jnp.bfloat16
small_eps = 1e-06
pieces = 2


def halves(x):
    hi = x.astype(BF16)
    lo = (x - hi.astype(F32)).astype(BF16)
    return hi, lo


def thirds(x):
    hi = x.astype(BF16)
    rest = x - hi.astype(F32)
    mid = rest.astype(BF16)
    lo = (rest - mid.astype(F32)).astype(BF16)
    return hi, mid, lo


def mm(a, b):
    return jnp.dot(a, b, preferred_element_type=F32)


def outward(k, n):
    return (n // 2 + ((k + 1) // 2) * (1 - 2 * (k % 2))) % n


def joined(x):
    hi = x.astype(BF16).astype(F32)
    return jnp.concatenate([hi, x - hi], axis=0).astype(BF16)


def kernel(
    sizes,
    near_hbm,
    side_ref,
    skel_ref,
    coup_hbm,
    basis_hbm,
    src_hbm,
    u_hbm,
    scale_ref,
    near_f,
    near_hi,
    near_lo,
    coup_f,
    basis_f,
    basis_w,
    nsel,
    a_v,
    acc_v,
    src_v,
    skel_out,
    skel_next,
    pick_w,
    wp,
    wc,
    u_in,
    u_out,
    n_v,
    p_in,
    p_out,
    e_in,
    e_out,
    w_sem,
    skel_sem,
    u_send,
    u_recv,
    p_send,
    p_recv,
    e_send,
    e_recv,
):
    ns, nt, nx, nz = sizes
    tile = src_v.shape[2]
    rows = src_v.shape[1]
    rank = skel_ref.shape[1]
    n = 2 * rank
    half = rows // 2
    slab = lax.axis_index("slab")
    me = lax.axis_index("trace")
    my_x, my_z = me // nz, me % nz
    has_next = slab < ns - 1
    has_prev = slab > 0
    from_far = slab > 1
    first = lax.broadcasted_iota(jnp.int32, (rank, n), 1) < rank

    basis_load = pltpu.make_async_copy(basis_hbm, basis_f, w_sem.at[0])
    coup_load = pltpu.make_async_copy(coup_hbm, coup_f, w_sem.at[1])
    src_load = pltpu.make_async_copy(src_hbm, src_v, w_sem.at[2])
    near_loads = [
        pltpu.make_async_copy(
            near_hbm.at[slot, part], near_f.at[slot, part], w_sem.at[3 + 2 * slot + part]
        )
        for slot in range(2)
        for part in range(2)
    ]
    for load in [src_load, coup_load, basis_load] + near_loads:
        load.start()

    spread = [
        (int(outward(k // nx, nz)), int(outward(k % nx, nx))) for k in range(nt)
    ]
    wrap_x = [lax.rem(my_x + dx, nx) * nz for dx in range(nx)]
    wrap_z = [lax.rem(my_z + dz, nz) for dz in range(nz)]

    def block_at(dz, dx):
        return wrap_x[dx] + wrap_z[dz]

    barrier = pltpu.get_barrier_semaphore()

    def greet(s, t):
        pl.semaphore_signal(barrier, inc=1, device_id=(s, t), device_id_type=MESH)

    @pl.when(has_prev)
    def _():
        for dz, dx in spread:
            greet(slab - 1, block_at(dz, dx))

    for dz, dx in spread[:-1]:
        greet(slab, block_at(dz, dx))

    @pl.when(has_next)
    def _():
        greet(slab + 1, me)

    twin = jnp.concatenate([skel_ref[...], skel_ref[...]], axis=1)
    skel_out[...] = jnp.broadcast_to(twin, skel_out.shape)
    side = side_ref[...]

    def choose(right, left):
        return jnp.where(jnp.broadcast_to(side, left.shape) > 0, right, left)

    def set_basis(b_re, b_im):
        top = jnp.concatenate([b_re, -b_im], axis=0)
        bottom = jnp.concatenate([b_im, b_re], axis=0)
        for j, m in enumerate((top, bottom)):
            hi, lo = halves(m)
            basis_w[:n, j * tile : (j + 1) * tile] = hi
            basis_w[n:, j * tile : (j + 1) * tile] = lo

    def far_part(coef):
        hi, lo = halves(coef)
        lhs = jnp.concatenate(
            [jnp.concatenate([hi, hi], axis=1), jnp.concatenate([lo, lo], axis=1)], axis=0
        )
        far = mm(lhs, basis_w[...])
        far = far[:rows] + far[rows:]
        return far[:, :tile], far[:, tile:]

    coup_load.wait()
    place = lax.broadcasted_iota(jnp.int32, (n, n), 1)

    @pl.loop(0, nt // 2, unroll=min(4, nt // 2))
    def _(t):
        at = pl.ds(pl.multiple_of(t * n, n), n)
        a = jnp.concatenate([coup_f[0, :, at], coup_f[1, :, at]], axis=0).T
        b = pltpu.roll(jnp.where(place < rank, a, -a), rank, 1)
        for odd in range(2):
            c = 2 * t + odd
            keep = jnp.logical_and(side + me != c, me != c).astype(F32)
            cx, cz = c // nz, c % nz
            for i, m in enumerate((a, b)):
                hi, lo = halves(m[odd * rank : (odd + 1) * rank] * keep)
                out_at = pl.ds(pl.multiple_of(cx * n + i * rank, rank), rank)
                wc[cz, out_at, :n] = hi
                wc[cz, out_at, n:] = lo

    basis_load.wait()
    set_basis(basis_f[0], basis_f[1])
    src_load.wait()

    pl.semaphore_wait(
        barrier, nt - 1 + nt * has_next.astype(jnp.int32) + has_prev.astype(jnp.int32)
    )

    skel_copy = pltpu.make_async_remote_copy(
        src_ref=skel_out,
        dst_ref=skel_next,
        send_sem=skel_sem.at[0],
        recv_sem=skel_sem.at[1],
        device_id=(slab - 1, me),
        device_id_type=MESH,
    )

    @pl.when(has_prev)
    def _():
        skel_copy.start()

    def send_three(src, dst, send, recv, cols):
        for i, shift in enumerate((nt - 1, 1, 0)):
            pltpu.make_async_remote_copy(
                src_ref=src,
                dst_ref=dst.at[i, :, :, cols],
                send_sem=send.at[i],
                recv_sem=recv.at[i],
                device_id=(slab + 1, (me + shift) % nt),
                device_id_type=MESH,
            ).start()

    def send_p(stream):
        for dz, dx in spread:
            pltpu.make_async_remote_copy(
                src_ref=p_out.at[stream],
                dst_ref=p_in.at[stream, dz, my_x],
                send_sem=p_send.at[stream],
                recv_sem=p_recv.at[stream, dz],
                device_id=(slab + 1, block_at(dz, dx)),
                device_id_type=MESH,
            ).start()

    def pick(x):
        parts = mm(jnp.concatenate(thirds(x), axis=0), pick_w[...])
        m = 2 * rows
        got = parts[:m] + parts[m : 2 * m] + parts[2 * m :]
        return jnp.where(first[:rows], got[:rows], got[rows:])

    @pl.when(slab == 0)
    def _():
        for piece in range(pieces):
            cols = slice(piece * tile // pieces, (piece + 1) * tile // pieces)
            send_three(src_v.at[:, :, cols], u_in, u_send.at[piece], u_recv.at[piece], cols)

        u_in[...] = jnp.zeros_like(u_in)
        p_in[...] = jnp.zeros_like(p_in)

    @pl.when(has_next)
    def _():
        skel_copy.wait_recv()
        unknown = lax.broadcasted_iota(jnp.int32, (tile, n), 0)
        pick_w[...] = (unknown == skel_next[:1, :]).astype(BF16)

    @pl.when(jnp.logical_not(has_next))
    def _():
        pick_w[...] = jnp.zeros_like(pick_w)

    @pl.when(slab == 0)
    def _():
        p_first = pick(src_v[...].reshape(2 * rows, tile))
        for stream in range(2):
            p_out[stream] = p_first[stream * half : (stream + 1) * half]
            send_p(stream)

    for slot in range(2):
        for part in range(2):
            near_loads[2 * slot + part].wait()

            @pl.loop(0, tile // 32)
            def _(i):
                at = pl.ds(pl.multiple_of(i * 32, 32), 32)
                hi, lo = halves(near_f[slot, part, at, :])
                near_hi[slot, part, at, :] = hi
                near_lo[slot, part, at, :] = lo

    b_all = basis_f[...].reshape(n, tile)
    picked = mm(jnp.concatenate(thirds(b_all), axis=0), pick_w[...])
    picked = picked[:n] + picked[n : 2 * n] + picked[2 * n :]
    s_re, s_im = picked[:rank], picked[rank:]
    s_mat = jnp.concatenate([jnp.where(first, s_re, s_im), jnp.where(first, -s_im, s_re)], axis=0)
    s_w = jnp.concatenate(halves(s_mat), axis=1)
    s_w = jnp.concatenate([s_w, s_w], axis=0)

    @pl.loop(0, nz, unroll=2)
    def _(z):
        prod = mm(wc[z], s_w)
        hi, lo = halves(prod[:, :n] + prod[:, n:])
        wp[z, :, :n] = hi
        wp[z, :, n:] = lo

    @pl.when(from_far)
    def _():
        in_first = lax.broadcasted_iota(jnp.int32, (tile, n), 1) < rank
        for slot in range(2):
            for i, w in enumerate((near_hi, near_lo)):
                re, im = mm(w[slot, 0], pick_w[...]), mm(w[slot, 1], pick_w[...])
                nsel[slot, :, i * n : (i + 1) * n] = jnp.where(in_first, re, im).astype(BF16)
        a_v[...] = pick(src_v[...].reshape(2 * rows, tile))

    def wait_u():
        for piece in range(pieces):
            cols = slice(piece * tile // pieces, (piece + 1) * tile // pieces)
            for i in range(3):
                part = u_in.at[i, :, :, cols]
                pltpu.make_async_copy(part, part, u_recv.at[piece, i]).wait()

    def incoming(slot):
        x = u_in[2] if slot == 0 else choose(u_in[0], u_in[1])
        return halves(x.reshape(2 * rows, tile))

    def near(cols):
        sums = [None, None]
        for slot in range(2):
            hi, lo = incoming(slot)
            both = jnp.concatenate([hi, lo], axis=0)
            for part in range(2):
                prod = mm(both, near_hi[slot, part, :, cols])
                term = prod[: 2 * rows] + prod[2 * rows :] + mm(hi, near_lo[slot, part, :, cols])
                sums[part] = term if slot == 0 else sums[part] + term
        n_v[0, :, cols] = sums[0][:rows] - sums[1][rows:] + src_v[0, :, cols]
        n_v[1, :, cols] = sums[1][:rows] + sums[0][rows:] + src_v[1, :, cols]

    @pl.when(jnp.logical_not(from_far))
    def _():
        @pl.when(has_prev)
        def _():
            wait_u()

        near(slice(0, tile))
        a_v[...] = pick(n_v[...].reshape(2 * rows, tile))

    order = [int(outward(k, nz)) for k in range(nz)][::-1]
    early = order[: nz // 2 + 1]
    late = order[nz // 2 + 1 :]

    def wait_p(stream, group):
        @pl.when(has_prev)
        def _():
            for dz in group:
                pltpu.make_async_copy(
                    p_in.at[stream, dz], p_in.at[stream, dz], p_recv.at[stream, dz]
                ).wait()

    def p_lhs(stream, dz):
        return joined(jnp.concatenate([p_in[stream, dz, x] for x in range(nx)], axis=1))

    def times(w, stream, group):
        total = None
        for dz in group:
            term = mm(p_lhs(stream, dz), w[(my_z - dz + nz) % nz])
            total = term if total is None else total + term
        return total

    def fold(acc):
        acc = acc[:half] + acc[half:]
        return acc[:, :n] + acc[:, n:]

    sends_on = jnp.logical_and(has_prev, has_next)

    def far_ahead(stream, group, start):
        @pl.when(sends_on)
        def _():
            term = times(wp, stream, group)
            acc_v[stream] = term if start else acc_v[stream] + term

    def emit(stream):
        p_out[stream] = a_v[stream * half : (stream + 1) * half] + fold(acc_v[stream])
        send_p(stream)

    wait_p(0, early)
    far_ahead(0, early, True)
    c_first = times(wc, 0, early)
    wait_p(0, late)
    far_ahead(0, late, False)

    @pl.when(slab == 1)
    def _():
        emit(0)

    c_first = fold(c_first + times(wc, 0, late))
    wait_p(1, early)
    far_ahead(1, early, True)
    c_second = times(wc, 1, early)

    @pl.when(from_far)
    def _():
        wait_u()

        @pl.when(has_next)
        def _():
            total = None
            for slot in range(2):
                term = mm(jnp.concatenate(incoming(slot), axis=0), nsel[slot])
                total = term if total is None else total + term
            total = total[: 2 * rows] + total[2 * rows :]
            total = total[:, :n] + total[:, n:]
            turned = pltpu.roll(total[rows:], rank, 1)
            a_v[...] += total[:rows] + jnp.where(first[:rows], -turned, turned)
            emit(0)

    wait_p(1, late)
    far_ahead(1, late, False)

    @pl.when(sends_on)
    def _():
        emit(1)

    coef = jnp.concatenate([c_first, fold(c_second + times(wc, 1, late))], axis=0)
    f_re, f_im = far_part(coef)
    u_out[0] = f_re
    u_out[1] = f_im
    for piece in range(pieces):
        cols = slice(piece * tile // pieces, (piece + 1) * tile // pieces)

        @pl.when(from_far)
        def _():
            near(cols)

        u_out[:, :, cols] += n_v[:, :, cols]

        @pl.when(sends_on)
        def _():
            send_three(u_out.at[:, :, cols], u_in, u_send.at[piece], u_recv.at[piece], cols)

    u_re, u_im = u_out[0], u_out[1]

    part_sum = jnp.sum(u_re * u_re + u_im * u_im, axis=1, keepdims=True)
    diag = (
        lax.broadcasted_iota(jnp.int32, (rows, 128), 0)
        == lax.broadcasted_iota(jnp.int32, (rows, 128), 1)
    ).astype(F32)
    e_out[...] = jnp.sum(part_sum * diag, axis=0, keepdims=True)

    for k, (dz, dx) in enumerate(spread[:-1]):
        pltpu.make_async_remote_copy(
            src_ref=e_out,
            dst_ref=e_in.at[k],
            send_sem=e_send,
            recv_sem=e_recv,
            device_id=(slab, block_at(dz, dx)),
            device_id_type=MESH,
        ).start()

    u_store = pltpu.make_async_copy(u_out, u_hbm, w_sem.at[7])
    u_store.start()

    pltpu.make_async_copy(e_in, e_in, e_recv).wait()
    total = e_out[...] + jnp.sum(e_in[...], axis=0)
    energy = jnp.sum(total * diag, axis=1, keepdims=True) / (2 * tile * nt)
    scale_ref[...] = jnp.broadcast_to(1.0 / jnp.sqrt(energy + small_eps), scale_ref.shape)

    u_store.wait()
    pltpu.make_async_copy(e_in, e_in, e_send).wait()

    @pl.when(has_next)
    def _():
        for piece in range(pieces):
            part = u_out.at[:, :, : tile // pieces]
            for i in range(3):
                pltpu.make_async_copy(part, part, u_send.at[piece, i]).wait()
        for stream in range(2):
            pltpu.make_async_copy(p_in.at[stream], p_in.at[stream], p_send.at[stream]).wait()

    @pl.when(has_prev)
    def _():
        skel_copy.wait_send()


def solution(mesh):
    ns, nt = mesh.shape["slab"], mesh.shape["trace"]
    nz = 8 if nt % 8 == 0 else nt
    nx = nt // nz

    def on_device(near_tiles, near_side, skeleton, far_coupling, far_basis, sources):
        rows, tile = sources.shape[2] * sources.shape[3], sources.shape[4]
        rank = skeleton.shape[2]
        any_space = pl.BlockSpec(memory_space=pl.ANY)
        vmem = pl.BlockSpec(memory_space=pltpu.VMEM)
        dma = pltpu.SemaphoreType.DMA
        u, scale = pl.pallas_call(
            functools.partial(kernel, (ns, nt, nx, nz)),
            out_shape=(
                jax.ShapeDtypeStruct((2, rows, tile), F32),
                jax.ShapeDtypeStruct((rows, tile), F32),
            ),
            in_specs=[any_space, vmem, vmem, any_space, any_space, any_space],
            out_specs=(any_space, vmem),
            scratch_shapes=[
                pltpu.VMEM((2, 2, tile, tile), F32),
                pltpu.VMEM((2, 2, tile, tile), BF16),
                pltpu.VMEM((2, 2, tile, tile), BF16),
                pltpu.VMEM((2, rank, nt * rank), F32),
                pltpu.VMEM((2, rank, tile), F32),
                pltpu.VMEM((4 * rank, 2 * tile), BF16),
                pltpu.VMEM((2, tile, 4 * rank), BF16),
                pltpu.VMEM((rows, 2 * rank), F32),
                pltpu.VMEM((2, rows, 4 * rank), F32),
                pltpu.VMEM((2, rows, tile), F32),
                pltpu.VMEM((8, 2 * rank), jnp.int32),
                pltpu.VMEM((8, 2 * rank), jnp.int32),
                pltpu.VMEM((tile, 2 * rank), BF16),
                pltpu.VMEM((nz, nx * 2 * rank, 4 * rank), BF16),
                pltpu.VMEM((nz, nx * 2 * rank, 4 * rank), BF16),
                pltpu.VMEM((3, 2, rows, tile), F32),
                pltpu.VMEM((2, rows, tile), F32),
                pltpu.VMEM((2, rows, tile), F32),
                pltpu.VMEM((2, nz, nx, rows // 2, 2 * rank), F32),
                pltpu.VMEM((2, rows // 2, 2 * rank), F32),
                pltpu.VMEM((nt - 1, 1, 128), F32),
                pltpu.VMEM((1, 128), F32),
                dma((8,)),
                dma((2,)),
                dma((pieces, 3)),
                dma((pieces, 3)),
                dma((2,)),
                dma((2, nz)),
                dma,
                dma,
            ],
            compiler_params=pltpu.CompilerParams(collective_id=0, has_side_effects=True),
        )(
            near_tiles[0],
            near_side,
            skeleton[0],
            far_coupling[0],
            far_basis[0],
            sources[0].reshape(2, rows, tile),
        )
        return (u * scale[None]).reshape(sources.shape)

    placed = (
        P("slab", None, None, None, "trace"),
        P("slab", "trace"),
        P("slab", "trace", None),
        P("slab", None, "trace", None),
        P("slab", None, None, "trace"),
        P("slab", None, None, None, "trace"),
    )
    return jax.shard_map(
        on_device,
        mesh=mesh,
        in_specs=placed,
        out_specs=P("slab", None, None, None, "trace"),
        check_vma=False,
    )
```

```python
import functools

import jax
import jax.numpy as jnp
from jax import lax
from jax.experimental import pallas as pl
from jax.experimental.pallas import tpu as pltpu
from jax.sharding import PartitionSpec as P

MESH = pl.DeviceIdType.MESH
F32 = jnp.float32
BF16 = jnp.bfloat16
small_eps = 1e-06
pieces = 2


def halves(x):
    hi = x.astype(BF16)
    lo = (x - hi.astype(F32)).astype(BF16)
    return hi, lo


def thirds(x):
    hi = x.astype(BF16)
    rest = x - hi.astype(F32)
    mid = rest.astype(BF16)
    lo = (rest - mid.astype(F32)).astype(BF16)
    return hi, mid, lo


def mm(a, b):
    return jnp.dot(a, b, preferred_element_type=F32)


def outward(k, n):
    return (n // 2 + ((k + 1) // 2) * (1 - 2 * (k % 2))) % n


def joined(x):
    hi = x.astype(BF16).astype(F32)
    return jnp.concatenate([hi, x - hi], axis=0).astype(BF16)


def kernel(
    sizes,
    near_hbm,
    side_ref,
    skel_ref,
    coup_hbm,
    basis_hbm,
    src_hbm,
    u_hbm,
    scale_ref,
    near_f,
    near_hi,
    near_lo,
    coup_f,
    basis_f,
    basis_w,
    nsel,
    a_v,
    acc_v,
    src_v,
    skel_out,
    skel_next,
    pick_w,
    wp,
    wc,
    u_in,
    u_out,
    n_v,
    p_in,
    p_out,
    e_in,
    e_out,
    w_sem,
    skel_sem,
    u_send,
    u_recv,
    p_send,
    p_recv,
    e_send,
    e_recv,
):
    ns, nt, nx, nz = sizes
    tile = src_v.shape[2]
    rows = src_v.shape[1]
    rank = skel_ref.shape[1]
    n = 2 * rank
    half = rows // 2
    slab = lax.axis_index("slab")
    me = lax.axis_index("trace")
    my_x, my_z = me // nz, me % nz
    has_next = slab < ns - 1
    has_prev = slab > 0
    from_far = slab > 1
    first = lax.broadcasted_iota(jnp.int32, (rank, n), 1) < rank

    basis_load = pltpu.make_async_copy(basis_hbm, basis_f, w_sem.at[0])
    coup_load = pltpu.make_async_copy(coup_hbm, coup_f, w_sem.at[1])
    src_load = pltpu.make_async_copy(src_hbm, src_v, w_sem.at[2])
    near_loads = [
        pltpu.make_async_copy(
            near_hbm.at[slot, part], near_f.at[slot, part], w_sem.at[3 + 2 * slot + part]
        )
        for slot in range(2)
        for part in range(2)
    ]
    for load in [src_load, coup_load, basis_load] + near_loads:
        load.start()

    spread = [
        (int(outward(k % nz, nz)), int(outward(k // nz, nx))) for k in range(nt)
    ]
    wrap_x = [lax.rem(my_x + dx, nx) * nz for dx in range(nx)]
    wrap_z = [lax.rem(my_z + dz, nz) for dz in range(nz)]

    def block_at(dz, dx):
        return wrap_x[dx] + wrap_z[dz]

    barrier = pltpu.get_barrier_semaphore()

    def greet(s, t):
        pl.semaphore_signal(barrier, inc=1, device_id=(s, t), device_id_type=MESH)

    @pl.when(has_prev)
    def _():
        for dz, dx in spread:
            greet(slab - 1, block_at(dz, dx))

    for dz, dx in spread[:-1]:
        greet(slab, block_at(dz, dx))

    @pl.when(has_next)
    def _():
        greet(slab + 1, me)

    twin = jnp.concatenate([skel_ref[...], skel_ref[...]], axis=1)
    skel_out[...] = jnp.broadcast_to(twin, skel_out.shape)
    side = side_ref[...]

    def choose(right, left):
        return jnp.where(jnp.broadcast_to(side, left.shape) > 0, right, left)

    def set_basis(b_re, b_im):
        top = jnp.concatenate([b_re, -b_im], axis=0)
        bottom = jnp.concatenate([b_im, b_re], axis=0)
        for j, m in enumerate((top, bottom)):
            hi, lo = halves(m)
            basis_w[:n, j * tile : (j + 1) * tile] = hi
            basis_w[n:, j * tile : (j + 1) * tile] = lo

    def far_part(coef):
        hi, lo = halves(coef)
        lhs = jnp.concatenate(
            [jnp.concatenate([hi, hi], axis=1), jnp.concatenate([lo, lo], axis=1)], axis=0
        )
        far = mm(lhs, basis_w[...])
        far = far[:rows] + far[rows:]
        return far[:, :tile], far[:, tile:]

    coup_load.wait()
    place = lax.broadcasted_iota(jnp.int32, (n, n), 1)

    @pl.loop(0, nt // 2, unroll=min(4, nt // 2))
    def _(t):
        at = pl.ds(pl.multiple_of(t * n, n), n)
        a = jnp.concatenate([coup_f[0, :, at], coup_f[1, :, at]], axis=0).T
        b = pltpu.roll(jnp.where(place < rank, a, -a), rank, 1)
        for odd in range(2):
            c = 2 * t + odd
            keep = jnp.logical_and(side + me != c, me != c).astype(F32)
            cx, cz = c // nz, c % nz
            for i, m in enumerate((a, b)):
                hi, lo = halves(m[odd * rank : (odd + 1) * rank] * keep)
                out_at = pl.ds(pl.multiple_of(cx * n + i * rank, rank), rank)
                wc[cz, out_at, :n] = hi
                wc[cz, out_at, n:] = lo

    basis_load.wait()
    set_basis(basis_f[0], basis_f[1])
    src_load.wait()

    pl.semaphore_wait(
        barrier, nt - 1 + nt * has_next.astype(jnp.int32) + has_prev.astype(jnp.int32)
    )

    skel_copy = pltpu.make_async_remote_copy(
        src_ref=skel_out,
        dst_ref=skel_next,
        send_sem=skel_sem.at[0],
        recv_sem=skel_sem.at[1],
        device_id=(slab - 1, me),
        device_id_type=MESH,
    )

    @pl.when(has_prev)
    def _():
        skel_copy.start()

    def send_three(src, dst, send, recv, cols):
        for i, shift in enumerate((nt - 1, 1, 0)):
            pltpu.make_async_remote_copy(
                src_ref=src,
                dst_ref=dst.at[i, :, :, cols],
                send_sem=send.at[i],
                recv_sem=recv.at[i],
                device_id=(slab + 1, (me + shift) % nt),
                device_id_type=MESH,
            ).start()

    def send_p(stream):
        for dz, dx in spread:
            pltpu.make_async_remote_copy(
                src_ref=p_out.at[stream],
                dst_ref=p_in.at[stream, dz, my_x],
                send_sem=p_send.at[stream],
                recv_sem=p_recv.at[stream, dz],
                device_id=(slab + 1, block_at(dz, dx)),
                device_id_type=MESH,
            ).start()

    def pick(x):
        parts = mm(jnp.concatenate(thirds(x), axis=0), pick_w[...])
        m = 2 * rows
        got = parts[:m] + parts[m : 2 * m] + parts[2 * m :]
        return jnp.where(first[:rows], got[:rows], got[rows:])

    @pl.when(slab == 0)
    def _():
        for piece in range(pieces):
            cols = slice(piece * tile // pieces, (piece + 1) * tile // pieces)
            send_three(src_v.at[:, :, cols], u_in, u_send.at[piece], u_recv.at[piece], cols)

        u_in[...] = jnp.zeros_like(u_in)
        p_in[...] = jnp.zeros_like(p_in)

    @pl.when(has_next)
    def _():
        skel_copy.wait_recv()
        unknown = lax.broadcasted_iota(jnp.int32, (tile, n), 0)
        pick_w[...] = (unknown == skel_next[:1, :]).astype(BF16)

    @pl.when(jnp.logical_not(has_next))
    def _():
        pick_w[...] = jnp.zeros_like(pick_w)

    @pl.when(slab == 0)
    def _():
        p_first = pick(src_v[...].reshape(2 * rows, tile))
        for stream in range(2):
            p_out[stream] = p_first[stream * half : (stream + 1) * half]
            send_p(stream)

    for slot in range(2):
        for part in range(2):
            near_loads[2 * slot + part].wait()

            @pl.loop(0, tile // 32)
            def _(i):
                at = pl.ds(pl.multiple_of(i * 32, 32), 32)
                hi, lo = halves(near_f[slot, part, at, :])
                near_hi[slot, part, at, :] = hi
                near_lo[slot, part, at, :] = lo

    b_all = basis_f[...].reshape(n, tile)
    picked = mm(jnp.concatenate(thirds(b_all), axis=0), pick_w[...])
    picked = picked[:n] + picked[n : 2 * n] + picked[2 * n :]
    s_re, s_im = picked[:rank], picked[rank:]
    s_mat = jnp.concatenate([jnp.where(first, s_re, s_im), jnp.where(first, -s_im, s_re)], axis=0)
    s_w = jnp.concatenate(halves(s_mat), axis=1)
    s_w = jnp.concatenate([s_w, s_w], axis=0)

    @pl.loop(0, nz, unroll=2)
    def _(z):
        prod = mm(wc[z], s_w)
        hi, lo = halves(prod[:, :n] + prod[:, n:])
        wp[z, :, :n] = hi
        wp[z, :, n:] = lo

    @pl.when(from_far)
    def _():
        in_first = lax.broadcasted_iota(jnp.int32, (tile, n), 1) < rank
        for slot in range(2):
            for i, w in enumerate((near_hi, near_lo)):
                re, im = mm(w[slot, 0], pick_w[...]), mm(w[slot, 1], pick_w[...])
                nsel[slot, :, i * n : (i + 1) * n] = jnp.where(in_first, re, im).astype(BF16)
        a_v[...] = pick(src_v[...].reshape(2 * rows, tile))

    def wait_u():
        for piece in range(pieces):
            cols = slice(piece * tile // pieces, (piece + 1) * tile // pieces)
            for i in range(3):
                part = u_in.at[i, :, :, cols]
                pltpu.make_async_copy(part, part, u_recv.at[piece, i]).wait()

    def incoming(slot):
        x = u_in[2] if slot == 0 else choose(u_in[0], u_in[1])
        return halves(x.reshape(2 * rows, tile))

    def near(cols):
        sums = [None, None]
        for slot in range(2):
            hi, lo = incoming(slot)
            both = jnp.concatenate([hi, lo], axis=0)
            for part in range(2):
                prod = mm(both, near_hi[slot, part, :, cols])
                term = prod[: 2 * rows] + prod[2 * rows :] + mm(hi, near_lo[slot, part, :, cols])
                sums[part] = term if slot == 0 else sums[part] + term
        n_v[0, :, cols] = sums[0][:rows] - sums[1][rows:] + src_v[0, :, cols]
        n_v[1, :, cols] = sums[1][:rows] + sums[0][rows:] + src_v[1, :, cols]

    @pl.when(jnp.logical_not(from_far))
    def _():
        @pl.when(has_prev)
        def _():
            wait_u()

        near(slice(0, tile))
        a_v[...] = pick(n_v[...].reshape(2 * rows, tile))

    order = [int(outward(k, nz)) for k in range(nz)][::-1]
    early = order[: nz // 2 + 1]
    late = order[nz // 2 + 1 :]

    def wait_p(stream, group):
        @pl.when(has_prev)
        def _():
            for dz in group:
                pltpu.make_async_copy(
                    p_in.at[stream, dz], p_in.at[stream, dz], p_recv.at[stream, dz]
                ).wait()

    def p_lhs(stream, dz):
        return joined(jnp.concatenate([p_in[stream, dz, x] for x in range(nx)], axis=1))

    def times(w, stream, group):
        total = None
        for dz in group:
            term = mm(p_lhs(stream, dz), w[(my_z - dz + nz) % nz])
            total = term if total is None else total + term
        return total

    def fold(acc):
        acc = acc[:half] + acc[half:]
        return acc[:, :n] + acc[:, n:]

    sends_on = jnp.logical_and(has_prev, has_next)

    def far_ahead(stream, group, start):
        @pl.when(sends_on)
        def _():
            term = times(wp, stream, group)
            acc_v[stream] = term if start else acc_v[stream] + term

    def emit(stream):
        p_out[stream] = a_v[stream * half : (stream + 1) * half] + fold(acc_v[stream])
        send_p(stream)

    wait_p(0, early)
    far_ahead(0, early, True)
    c_first = times(wc, 0, early)
    wait_p(0, late)
    far_ahead(0, late, False)

    @pl.when(slab == 1)
    def _():
        emit(0)

    c_first = fold(c_first + times(wc, 0, late))
    wait_p(1, early)
    far_ahead(1, early, True)
    c_second = times(wc, 1, early)

    @pl.when(from_far)
    def _():
        wait_u()

        @pl.when(has_next)
        def _():
            total = None
            for slot in range(2):
                term = mm(jnp.concatenate(incoming(slot), axis=0), nsel[slot])
                total = term if total is None else total + term
            total = total[: 2 * rows] + total[2 * rows :]
            total = total[:, :n] + total[:, n:]
            turned = pltpu.roll(total[rows:], rank, 1)
            a_v[...] += total[:rows] + jnp.where(first[:rows], -turned, turned)
            emit(0)

    wait_p(1, late)
    far_ahead(1, late, False)

    @pl.when(sends_on)
    def _():
        emit(1)

    coef = jnp.concatenate([c_first, fold(c_second + times(wc, 1, late))], axis=0)
    f_re, f_im = far_part(coef)
    u_out[0] = f_re
    u_out[1] = f_im
    for piece in range(pieces):
        cols = slice(piece * tile // pieces, (piece + 1) * tile // pieces)

        @pl.when(from_far)
        def _():
            near(cols)

        u_out[:, :, cols] += n_v[:, :, cols]

        @pl.when(sends_on)
        def _():
            send_three(u_out.at[:, :, cols], u_in, u_send.at[piece], u_recv.at[piece], cols)

    u_re, u_im = u_out[0], u_out[1]

    part_sum = jnp.sum(u_re * u_re + u_im * u_im, axis=1, keepdims=True)
    diag = (
        lax.broadcasted_iota(jnp.int32, (rows, 128), 0)
        == lax.broadcasted_iota(jnp.int32, (rows, 128), 1)
    ).astype(F32)
    e_out[...] = jnp.sum(part_sum * diag, axis=0, keepdims=True)

    for k, (dz, dx) in enumerate(spread[:-1]):
        pltpu.make_async_remote_copy(
            src_ref=e_out,
            dst_ref=e_in.at[k],
            send_sem=e_send,
            recv_sem=e_recv,
            device_id=(slab, block_at(dz, dx)),
            device_id_type=MESH,
        ).start()

    u_store = pltpu.make_async_copy(u_out, u_hbm, w_sem.at[7])
    u_store.start()

    pltpu.make_async_copy(e_in, e_in, e_recv).wait()
    total = e_out[...] + jnp.sum(e_in[...], axis=0)
    energy = jnp.sum(total * diag, axis=1, keepdims=True) / (2 * tile * nt)
    scale_ref[...] = jnp.broadcast_to(1.0 / jnp.sqrt(energy + small_eps), scale_ref.shape)

    u_store.wait()
    pltpu.make_async_copy(e_in, e_in, e_send).wait()

    @pl.when(has_next)
    def _():
        for piece in range(pieces):
            part = u_out.at[:, :, : tile // pieces]
            for i in range(3):
                pltpu.make_async_copy(part, part, u_send.at[piece, i]).wait()
        for stream in range(2):
            pltpu.make_async_copy(p_in.at[stream], p_in.at[stream], p_send.at[stream]).wait()

    @pl.when(has_prev)
    def _():
        skel_copy.wait_send()


def solution(mesh):
    ns, nt = mesh.shape["slab"], mesh.shape["trace"]
    nz = 8 if nt % 8 == 0 else nt
    nx = nt // nz

    def on_device(near_tiles, near_side, skeleton, far_coupling, far_basis, sources):
        rows, tile = sources.shape[2] * sources.shape[3], sources.shape[4]
        rank = skeleton.shape[2]
        any_space = pl.BlockSpec(memory_space=pl.ANY)
        vmem = pl.BlockSpec(memory_space=pltpu.VMEM)
        dma = pltpu.SemaphoreType.DMA
        u, scale = pl.pallas_call(
            functools.partial(kernel, (ns, nt, nx, nz)),
            out_shape=(
                jax.ShapeDtypeStruct((2, rows, tile), F32),
                jax.ShapeDtypeStruct((rows, tile), F32),
            ),
            in_specs=[any_space, vmem, vmem, any_space, any_space, any_space],
            out_specs=(any_space, vmem),
            scratch_shapes=[
                pltpu.VMEM((2, 2, tile, tile), F32),
                pltpu.VMEM((2, 2, tile, tile), BF16),
                pltpu.VMEM((2, 2, tile, tile), BF16),
                pltpu.VMEM((2, rank, nt * rank), F32),
                pltpu.VMEM((2, rank, tile), F32),
                pltpu.VMEM((4 * rank, 2 * tile), BF16),
                pltpu.VMEM((2, tile, 4 * rank), BF16),
                pltpu.VMEM((rows, 2 * rank), F32),
                pltpu.VMEM((2, rows, 4 * rank), F32),
                pltpu.VMEM((2, rows, tile), F32),
                pltpu.VMEM((8, 2 * rank), jnp.int32),
                pltpu.VMEM((8, 2 * rank), jnp.int32),
                pltpu.VMEM((tile, 2 * rank), BF16),
                pltpu.VMEM((nz, nx * 2 * rank, 4 * rank), BF16),
                pltpu.VMEM((nz, nx * 2 * rank, 4 * rank), BF16),
                pltpu.VMEM((3, 2, rows, tile), F32),
                pltpu.VMEM((2, rows, tile), F32),
                pltpu.VMEM((2, rows, tile), F32),
                pltpu.VMEM((2, nz, nx, rows // 2, 2 * rank), F32),
                pltpu.VMEM((2, rows // 2, 2 * rank), F32),
                pltpu.VMEM((nt - 1, 1, 128), F32),
                pltpu.VMEM((1, 128), F32),
                dma((8,)),
                dma((2,)),
                dma((pieces, 3)),
                dma((pieces, 3)),
                dma((2,)),
                dma((2, nz)),
                dma,
                dma,
            ],
            compiler_params=pltpu.CompilerParams(collective_id=0, has_side_effects=True),
        )(
            near_tiles[0],
            near_side,
            skeleton[0],
            far_coupling[0],
            far_basis[0],
            sources[0].reshape(2, rows, tile),
        )
        return (u * scale[None]).reshape(sources.shape)

    placed = (
        P("slab", None, None, None, "trace"),
        P("slab", "trace"),
        P("slab", "trace", None),
        P("slab", None, "trace", None),
        P("slab", None, None, "trace"),
        P("slab", None, None, None, "trace"),
    )
    return jax.shard_map(
        on_device,
        mesh=mesh,
        in_specs=placed,
        out_specs=P("slab", None, None, None, "trace"),
        check_vma=False,
    )
```

```python
import functools

import jax
import jax.numpy as jnp
from jax import lax
from jax.experimental import pallas as pl
from jax.experimental.pallas import tpu as pltpu
from jax.sharding import PartitionSpec as P

MESH = pl.DeviceIdType.MESH
F32 = jnp.float32
BF16 = jnp.bfloat16
small_eps = 1e-06
pieces = 2


def halves(x):
    hi = x.astype(BF16)
    lo = (x - hi.astype(F32)).astype(BF16)
    return hi, lo


def thirds(x):
    hi = x.astype(BF16)
    rest = x - hi.astype(F32)
    mid = rest.astype(BF16)
    lo = (rest - mid.astype(F32)).astype(BF16)
    return hi, mid, lo


def mm(a, b):
    return jnp.dot(a, b, preferred_element_type=F32)


def outward(k, n):
    return (n // 2 + ((k + 1) // 2) * (1 - 2 * (k % 2))) % n


def joined(x):
    hi = x.astype(BF16).astype(F32)
    return jnp.concatenate([hi, x - hi], axis=0).astype(BF16)


def kernel(
    sizes,
    near_hbm,
    side_ref,
    skel_ref,
    coup_hbm,
    basis_hbm,
    src_hbm,
    u_hbm,
    scale_ref,
    near_f,
    near_hi,
    near_lo,
    coup_f,
    basis_f,
    basis_w,
    nsel,
    a_v,
    acc_v,
    src_v,
    skel_out,
    skel_next,
    pick_w,
    wp,
    wc,
    u_in,
    u_out,
    n_v,
    p_in,
    p_out,
    e_in,
    e_out,
    w_sem,
    skel_sem,
    u_send,
    u_recv,
    p_send,
    p_recv,
    e_send,
    e_recv,
):
    ns, nt, nx, nz = sizes
    tile = src_v.shape[2]
    rows = src_v.shape[1]
    rank = skel_ref.shape[1]
    n = 2 * rank
    half = rows // 2
    slab = lax.axis_index("slab")
    me = lax.axis_index("trace")
    my_x, my_z = me // nz, me % nz
    has_next = slab < ns - 1
    has_prev = slab > 0
    from_far = slab > 1
    first = lax.broadcasted_iota(jnp.int32, (rank, n), 1) < rank

    basis_load = pltpu.make_async_copy(basis_hbm, basis_f, w_sem.at[0])
    coup_load = pltpu.make_async_copy(coup_hbm, coup_f, w_sem.at[1])
    src_load = pltpu.make_async_copy(src_hbm, src_v, w_sem.at[2])
    near_loads = [
        pltpu.make_async_copy(
            near_hbm.at[slot, part], near_f.at[slot, part], w_sem.at[3 + 2 * slot + part]
        )
        for slot in range(2)
        for part in range(2)
    ]
    for load in [src_load, coup_load, basis_load] + near_loads:
        load.start()

    spread = [
        (int(outward(k % nz, nz)), int(outward(k // nz, nx))) for k in range(nt)
    ]
    wrap_x = [lax.rem(my_x + dx, nx) * nz for dx in range(nx)]
    wrap_z = [lax.rem(my_z + dz, nz) for dz in range(nz)]

    def block_at(dz, dx):
        return wrap_x[dx] + wrap_z[dz]

    barrier = pltpu.get_barrier_semaphore()

    def greet(s, t):
        pl.semaphore_signal(barrier, inc=1, device_id=(s, t), device_id_type=MESH)

    @pl.when(has_prev)
    def _():
        for dz, dx in spread:
            greet(slab - 1, block_at(dz, dx))

    for dz, dx in spread[:-1]:
        greet(slab, block_at(dz, dx))

    @pl.when(has_next)
    def _():
        greet(slab + 1, me)

    twin = jnp.concatenate([skel_ref[...], skel_ref[...]], axis=1)
    skel_out[...] = jnp.broadcast_to(twin, skel_out.shape)
    side = side_ref[...]

    def choose(right, left):
        return jnp.where(jnp.broadcast_to(side, left.shape) > 0, right, left)

    def set_basis(b_re, b_im):
        top = jnp.concatenate([b_re, -b_im], axis=0)
        bottom = jnp.concatenate([b_im, b_re], axis=0)
        for j, m in enumerate((top, bottom)):
            hi, lo = halves(m)
            basis_w[:n, j * tile : (j + 1) * tile] = hi
            basis_w[n:, j * tile : (j + 1) * tile] = lo

    def far_part(coef):
        hi, lo = halves(coef)
        lhs = jnp.concatenate(
            [jnp.concatenate([hi, hi], axis=1), jnp.concatenate([lo, lo], axis=1)], axis=0
        )
        far = mm(lhs, basis_w[...])
        far = far[:rows] + far[rows:]
        return far[:, :tile], far[:, tile:]

    coup_load.wait()
    place = lax.broadcasted_iota(jnp.int32, (n, n), 1)

    @pl.loop(0, nt // 2, unroll=min(4, nt // 2))
    def _(t):
        at = pl.ds(pl.multiple_of(t * n, n), n)
        a = jnp.concatenate([coup_f[0, :, at], coup_f[1, :, at]], axis=0).T
        b = pltpu.roll(jnp.where(place < rank, a, -a), rank, 1)
        for odd in range(2):
            c = 2 * t + odd
            keep = jnp.logical_and(side + me != c, me != c).astype(F32)
            cx, cz = c // nz, c % nz
            for i, m in enumerate((a, b)):
                hi, lo = halves(m[odd * rank : (odd + 1) * rank] * keep)
                out_at = pl.ds(pl.multiple_of(cx * n + i * rank, rank), rank)
                wc[cz, out_at, :n] = hi
                wc[cz, out_at, n:] = lo

    basis_load.wait()
    set_basis(basis_f[0], basis_f[1])
    src_load.wait()

    pl.semaphore_wait(
        barrier, nt - 1 + nt * has_next.astype(jnp.int32) + has_prev.astype(jnp.int32)
    )

    skel_copy = pltpu.make_async_remote_copy(
        src_ref=skel_out,
        dst_ref=skel_next,
        send_sem=skel_sem.at[0],
        recv_sem=skel_sem.at[1],
        device_id=(slab - 1, me),
        device_id_type=MESH,
    )

    @pl.when(has_prev)
    def _():
        skel_copy.start()

    def send_three(src, dst, send, recv, cols):
        for i, shift in enumerate((nt - 1, 1, 0)):
            pltpu.make_async_remote_copy(
                src_ref=src,
                dst_ref=dst.at[i, :, :, cols],
                send_sem=send.at[i],
                recv_sem=recv.at[i],
                device_id=(slab + 1, (me + shift) % nt),
                device_id_type=MESH,
            ).start()

    def send_p(stream):
        for dz, dx in spread:
            pltpu.make_async_remote_copy(
                src_ref=p_out.at[stream],
                dst_ref=p_in.at[stream, dz, my_x],
                send_sem=p_send.at[stream],
                recv_sem=p_recv.at[stream, dz],
                device_id=(slab + 1, block_at(dz, dx)),
                device_id_type=MESH,
            ).start()

    def pick(x):
        parts = mm(jnp.concatenate(thirds(x), axis=0), pick_w[...])
        m = 2 * rows
        got = parts[:m] + parts[m : 2 * m] + parts[2 * m :]
        return jnp.where(first[:rows], got[:rows], got[rows:])

    @pl.when(slab == 0)
    def _():
        for piece in range(pieces):
            cols = slice(piece * tile // pieces, (piece + 1) * tile // pieces)
            send_three(src_v.at[:, :, cols], u_in, u_send.at[piece], u_recv.at[piece], cols)

        u_in[...] = jnp.zeros_like(u_in)
        p_in[...] = jnp.zeros_like(p_in)

    @pl.when(has_next)
    def _():
        skel_copy.wait_recv()
        unknown = lax.broadcasted_iota(jnp.int32, (tile, n), 0)
        pick_w[...] = (unknown == skel_next[:1, :]).astype(BF16)

    @pl.when(jnp.logical_not(has_next))
    def _():
        pick_w[...] = jnp.zeros_like(pick_w)

    @pl.when(slab == 0)
    def _():
        p_first = pick(src_v[...].reshape(2 * rows, tile))
        for stream in range(2):
            p_out[stream] = p_first[stream * half : (stream + 1) * half]
            send_p(stream)

    for slot in range(2):
        for part in range(2):
            near_loads[2 * slot + part].wait()

            @pl.loop(0, tile // 32)
            def _(i):
                at = pl.ds(pl.multiple_of(i * 32, 32), 32)
                hi, lo = halves(near_f[slot, part, at, :])
                near_hi[slot, part, at, :] = hi
                near_lo[slot, part, at, :] = lo

    b_all = basis_f[...].reshape(n, tile)
    picked = mm(jnp.concatenate(thirds(b_all), axis=0), pick_w[...])
    picked = picked[:n] + picked[n : 2 * n] + picked[2 * n :]
    s_re, s_im = picked[:rank], picked[rank:]
    s_mat = jnp.concatenate([jnp.where(first, s_re, s_im), jnp.where(first, -s_im, s_re)], axis=0)
    s_w = jnp.concatenate(halves(s_mat), axis=1)
    s_w = jnp.concatenate([s_w, s_w], axis=0)

    @pl.loop(0, nz, unroll=2)
    def _(z):
        prod = mm(wc[z], s_w)
        hi, lo = halves(prod[:, :n] + prod[:, n:])
        wp[z, :, :n] = hi
        wp[z, :, n:] = lo

    @pl.when(from_far)
    def _():
        in_first = lax.broadcasted_iota(jnp.int32, (tile, n), 1) < rank
        for slot in range(2):
            for i, w in enumerate((near_hi, near_lo)):
                re, im = mm(w[slot, 0], pick_w[...]), mm(w[slot, 1], pick_w[...])
                nsel[slot, :, i * n : (i + 1) * n] = jnp.where(in_first, re, im).astype(BF16)
        a_v[...] = pick(src_v[...].reshape(2 * rows, tile))

    def piece_at(piece):
        return slice(piece * tile // pieces, (piece + 1) * tile // pieces)

    def wait_u(piece):
        for i in range(3):
            part = u_in.at[i, :, :, piece_at(piece)]
            pltpu.make_async_copy(part, part, u_recv.at[piece, i]).wait()

    def incoming(slot, span):
        def block(i):
            return u_in[i, :, :, span].reshape(2 * rows, span.stop - span.start)

        return halves(block(2) if slot == 0 else choose(block(0), block(1)))

    def near(span, cols):
        sums = [None, None]
        for slot in range(2):
            hi, lo = incoming(slot, span)
            both = jnp.concatenate([hi, lo], axis=0)
            for part in range(2):
                prod = mm(both, near_hi[slot, part, span, cols])
                term = prod[: 2 * rows] + prod[2 * rows :] + mm(hi, near_lo[slot, part, span, cols])
                sums[part] = term if slot == 0 else sums[part] + term
        return sums[0][:rows] - sums[1][rows:], sums[1][:rows] + sums[0][rows:]

    @pl.when(jnp.logical_not(from_far))
    def _():
        @pl.when(has_prev)
        def _():
            for piece in range(pieces):
                wait_u(piece)

        n_re, n_im = near(slice(0, tile), slice(0, tile))
        n_v[0] = n_re + src_v[0]
        n_v[1] = n_im + src_v[1]
        a_v[...] = pick(n_v[...].reshape(2 * rows, tile))

    order = [int(outward(k, nz)) for k in range(nz)][::-1]
    early = order[: nz // 2 + 1]
    late = order[nz // 2 + 1 :]

    def wait_p(stream, group):
        @pl.when(has_prev)
        def _():
            for dz in group:
                pltpu.make_async_copy(
                    p_in.at[stream, dz], p_in.at[stream, dz], p_recv.at[stream, dz]
                ).wait()

    def p_lhs(stream, dz):
        return joined(jnp.concatenate([p_in[stream, dz, x] for x in range(nx)], axis=1))

    def times(w, stream, group):
        total = None
        for dz in group:
            term = mm(p_lhs(stream, dz), w[(my_z - dz + nz) % nz])
            total = term if total is None else total + term
        return total

    def fold(acc):
        acc = acc[:half] + acc[half:]
        return acc[:, :n] + acc[:, n:]

    sends_on = jnp.logical_and(has_prev, has_next)

    def far_ahead(stream, group, start):
        @pl.when(sends_on)
        def _():
            term = times(wp, stream, group)
            acc_v[stream] = term if start else acc_v[stream] + term

    def emit(stream):
        p_out[stream] = a_v[stream * half : (stream + 1) * half] + fold(acc_v[stream])
        send_p(stream)

    wait_p(0, early)
    far_ahead(0, early, True)
    c_first = times(wc, 0, early)
    wait_p(0, late)
    far_ahead(0, late, False)

    @pl.when(slab == 1)
    def _():
        emit(0)

    c_first = fold(c_first + times(wc, 0, late))
    wait_p(1, early)
    far_ahead(1, early, True)
    c_second = times(wc, 1, early)

    @pl.when(from_far)
    def _():
        for piece in range(pieces):
            span = piece_at(piece)
            wait_u(piece)

            @pl.when(has_next)
            def _():
                total = None
                for slot in range(2):
                    lhs = jnp.concatenate(incoming(slot, span), axis=0)
                    term = mm(lhs, nsel[slot, span])
                    total = term if total is None else total + term
                total = total[: 2 * rows] + total[2 * rows :]
                total = total[:, :n] + total[:, n:]
                turned = pltpu.roll(total[rows:], rank, 1)
                a_v[...] += total[:rows] + jnp.where(first[:rows], -turned, turned)
                if piece == pieces - 1:
                    emit(0)

    wait_p(1, late)
    far_ahead(1, late, False)

    @pl.when(sends_on)
    def _():
        emit(1)

    coef = jnp.concatenate([c_first, fold(c_second + times(wc, 1, late))], axis=0)
    f_re, f_im = far_part(coef)
    u_out[0] = f_re
    u_out[1] = f_im
    for piece in range(pieces):
        cols = slice(piece * tile // pieces, (piece + 1) * tile // pieces)

        @pl.when(from_far)
        def _():
            n_re, n_im = near(slice(0, tile), cols)
            n_v[0, :, cols] = n_re + src_v[0, :, cols]
            n_v[1, :, cols] = n_im + src_v[1, :, cols]

        u_out[:, :, cols] += n_v[:, :, cols]

        @pl.when(sends_on)
        def _():
            send_three(u_out.at[:, :, cols], u_in, u_send.at[piece], u_recv.at[piece], cols)

    u_re, u_im = u_out[0], u_out[1]

    part_sum = jnp.sum(u_re * u_re + u_im * u_im, axis=1, keepdims=True)
    diag = (
        lax.broadcasted_iota(jnp.int32, (rows, 128), 0)
        == lax.broadcasted_iota(jnp.int32, (rows, 128), 1)
    ).astype(F32)
    e_out[...] = jnp.sum(part_sum * diag, axis=0, keepdims=True)

    for k, (dz, dx) in enumerate(spread[:-1]):
        pltpu.make_async_remote_copy(
            src_ref=e_out,
            dst_ref=e_in.at[k],
            send_sem=e_send,
            recv_sem=e_recv,
            device_id=(slab, block_at(dz, dx)),
            device_id_type=MESH,
        ).start()

    u_store = pltpu.make_async_copy(u_out, u_hbm, w_sem.at[7])
    u_store.start()

    pltpu.make_async_copy(e_in, e_in, e_recv).wait()
    total = e_out[...] + jnp.sum(e_in[...], axis=0)
    energy = jnp.sum(total * diag, axis=1, keepdims=True) / (2 * tile * nt)
    scale_ref[...] = jnp.broadcast_to(1.0 / jnp.sqrt(energy + small_eps), scale_ref.shape)

    u_store.wait()
    pltpu.make_async_copy(e_in, e_in, e_send).wait()

    @pl.when(has_next)
    def _():
        for piece in range(pieces):
            part = u_out.at[:, :, : tile // pieces]
            for i in range(3):
                pltpu.make_async_copy(part, part, u_send.at[piece, i]).wait()
        for stream in range(2):
            pltpu.make_async_copy(p_in.at[stream], p_in.at[stream], p_send.at[stream]).wait()

    @pl.when(has_prev)
    def _():
        skel_copy.wait_send()


def solution(mesh):
    ns, nt = mesh.shape["slab"], mesh.shape["trace"]
    nz = 8 if nt % 8 == 0 else nt
    nx = nt // nz

    def on_device(near_tiles, near_side, skeleton, far_coupling, far_basis, sources):
        rows, tile = sources.shape[2] * sources.shape[3], sources.shape[4]
        rank = skeleton.shape[2]
        any_space = pl.BlockSpec(memory_space=pl.ANY)
        vmem = pl.BlockSpec(memory_space=pltpu.VMEM)
        dma = pltpu.SemaphoreType.DMA
        u, scale = pl.pallas_call(
            functools.partial(kernel, (ns, nt, nx, nz)),
            out_shape=(
                jax.ShapeDtypeStruct((2, rows, tile), F32),
                jax.ShapeDtypeStruct((rows, tile), F32),
            ),
            in_specs=[any_space, vmem, vmem, any_space, any_space, any_space],
            out_specs=(any_space, vmem),
            scratch_shapes=[
                pltpu.VMEM((2, 2, tile, tile), F32),
                pltpu.VMEM((2, 2, tile, tile), BF16),
                pltpu.VMEM((2, 2, tile, tile), BF16),
                pltpu.VMEM((2, rank, nt * rank), F32),
                pltpu.VMEM((2, rank, tile), F32),
                pltpu.VMEM((4 * rank, 2 * tile), BF16),
                pltpu.VMEM((2, tile, 4 * rank), BF16),
                pltpu.VMEM((rows, 2 * rank), F32),
                pltpu.VMEM((2, rows, 4 * rank), F32),
                pltpu.VMEM((2, rows, tile), F32),
                pltpu.VMEM((8, 2 * rank), jnp.int32),
                pltpu.VMEM((8, 2 * rank), jnp.int32),
                pltpu.VMEM((tile, 2 * rank), BF16),
                pltpu.VMEM((nz, nx * 2 * rank, 4 * rank), BF16),
                pltpu.VMEM((nz, nx * 2 * rank, 4 * rank), BF16),
                pltpu.VMEM((3, 2, rows, tile), F32),
                pltpu.VMEM((2, rows, tile), F32),
                pltpu.VMEM((2, rows, tile), F32),
                pltpu.VMEM((2, nz, nx, rows // 2, 2 * rank), F32),
                pltpu.VMEM((2, rows // 2, 2 * rank), F32),
                pltpu.VMEM((nt - 1, 1, 128), F32),
                pltpu.VMEM((1, 128), F32),
                dma((8,)),
                dma((2,)),
                dma((pieces, 3)),
                dma((pieces, 3)),
                dma((2,)),
                dma((2, nz)),
                dma,
                dma,
            ],
            compiler_params=pltpu.CompilerParams(collective_id=0, has_side_effects=True),
        )(
            near_tiles[0],
            near_side,
            skeleton[0],
            far_coupling[0],
            far_basis[0],
            sources[0].reshape(2, rows, tile),
        )
        return (u * scale[None]).reshape(sources.shape)

    placed = (
        P("slab", None, None, None, "trace"),
        P("slab", "trace"),
        P("slab", "trace", None),
        P("slab", None, "trace", None),
        P("slab", None, None, "trace"),
        P("slab", None, None, None, "trace"),
    )
    return jax.shard_map(
        on_device,
        mesh=mesh,
        in_specs=placed,
        out_specs=P("slab", None, None, None, "trace"),
        check_vma=False,
    )
```
